768 devices in a mesh: tower: 8 (over y_hi, x), shard: 96 (over z, y_lo, core).
Axes of the slice: x: 4, y: 8 (y_hi: 2, y_lo: 4; y = y_hi * 4 + y_lo), z: 12, core: 2. Of those that a mesh axis runs over, the one named last changes fastest.
Arguments:
- out_grad: bfloat16 [24576, 2048], P(('tower', 'shard')), may hold values from -6 to 6
- pooled: bfloat16 [8, 24576, 2048], P('tower', 'shard'), may hold values from -6 to 6
- down_proj: bfloat16 [8, 2048, 256], P('tower'), may hold values from -0.125 to 0.125
- up_proj: bfloat16 [8, 256, 2048], P('tower'), may hold values from -0.375 to 0.375
- cross_bias: float32 [8, 2048], P('tower'), may hold values from -3 to 3
- out_proj: bfloat16 [8, 2048, 256], P('tower'), may hold values from -0.125 to 0.125
- assign: int32 [128], replicated, may hold values from 0 to 127, each once
Outputs:
- feature_grad: bfloat16 [24576, 16384], P(('tower', 'shard'))
- weight_grad: float32 [8, 768, 2048], P('tower', 'shard')
- bias_grad: float32 [8, 2048], P('tower')
The draws below stay inside these ranges and needn't reach their ends.
Inputs may be any that keep to these rules, and one draw needn't show every extreme that they name: `assign`: slot k of the 128 slots belongs to tower k // 16; every feature sits in exactly one slot.
All inputs are finite; a program needn't handle non-finite values.
Results may differ from the reference program's by a relative error of at most 0.01.
Values may be sent and summed in bfloat16 or wider, within the bound.
A program may use at most 32 MiB of HBM per device.

```python
import math
import jax
import jax.numpy as jnp
from jax import lax

EMB = 128
R = 256
OUT = 256
ROWS_DEV = 32
W = 2048
TOWERS = 8
FEATURES = 128
ROWS = 24576
N_TOWER = 8
N_SHARD = 96


def block_scale(rng, shape, split, low, high):
    def one(axis_at, blocks):
        heights = jax.random.uniform(jax.random.fold_in(jax.random.fold_in(rng, 6), axis_at), (blocks,), jnp.float32, low / len(split), high / len(split))
        return jnp.repeat(jnp.exp(heights), shape[axis_at] // blocks).reshape((-1,) + (1,) * (len(shape) - axis_at - 1))

    gain = one(*split[0])
    for cut in split[1:]:
        gain = gain * one(*cut)
    return gain


def bell_draw(own_key, extent, scale, bound, cuts=(), held_as=jnp.bfloat16):
    result = jax.random.normal(own_key, extent, jnp.float32) * scale
    if len(cuts) > 0:
        result = block_scale(own_key, extent, cuts, -0.22, 0.18) * result
    return jnp.clip(result, min=-bound, max=bound).astype(held_as)


def setup_inputs(seed: int = 0) -> dict:
    key_list = jax.random.split(jax.random.key(seed), 8)
    out_grad = bell_draw(key_list[0], (ROWS, TOWERS * OUT), 1.0, 6.0, ((0, 768),))
    pooled = bell_draw(key_list[1], (TOWERS, ROWS, W), 1.0, 6.0, ((0, 8), (1, 96)))
    down_proj = bell_draw(key_list[2], (TOWERS, W, R), W ** -0.5, 0.125, ((0, 8),))
    up_proj = bell_draw(key_list[3], (TOWERS, R, W), R ** -0.5, 0.375, ((0, 8),))
    cross_bias = bell_draw(key_list[4], (TOWERS, W), 0.5, 3.0, ((0, 8),), jnp.float32)
    out_proj = bell_draw(key_list[5], (TOWERS, W, OUT), W ** -0.5, 0.125, ((0, 8),))
    assign = jax.random.permutation(key_list[6], FEATURES).astype(jnp.int32)
    return {"out_grad": out_grad, "pooled": pooled, "down_proj": down_proj, "up_proj": up_proj, "cross_bias": cross_bias, "out_proj": out_proj, "assign": assign}


def tower_backward(args):
    feature_in, grad_out, w_down, w_up, bias_row, w_out = args
    hidden_low = jnp.dot(feature_in, w_down, preferred_element_type=jnp.float32).astype(jnp.bfloat16)
    gate_full = jnp.dot(hidden_low, w_up, preferred_element_type=jnp.float32) + bias_row[None, :]
    factor = gate_full + 1.0
    inputs_wide = feature_in.astype(jnp.float32)
    crossed = (inputs_wide * factor).astype(jnp.bfloat16)
    grad_crossed = jnp.dot(grad_out, w_out.T, preferred_element_type=jnp.float32).astype(jnp.bfloat16)
    grad_gate = grad_crossed.astype(jnp.float32) * inputs_wide
    bias_part = lax.optimization_barrier(jnp.sum(grad_gate, axis=0))
    grad_gate_low = grad_gate.astype(jnp.bfloat16)
    grad_hidden = jnp.dot(grad_gate_low, w_up.T, preferred_element_type=jnp.float32).astype(jnp.bfloat16)
    grad_inputs = (grad_crossed.astype(jnp.float32) * factor + jnp.dot(grad_hidden, w_down.T, preferred_element_type=jnp.float32)).astype(jnp.bfloat16)
    stacked = jnp.concatenate([jnp.einsum('nr,nw->rw', grad_hidden.astype(jnp.float32), inputs_wide), jnp.einsum('nr,nw->rw', hidden_low.astype(jnp.float32), grad_gate_low.astype(jnp.float32)), jnp.einsum('nr,nw->rw', grad_out.astype(jnp.float32), crossed.astype(jnp.float32))], axis=0)
    return (grad_inputs, stacked, bias_part)

def reference(out_grad, pooled, down_proj, up_proj, cross_bias, out_proj, assign):
    regroup = out_grad.reshape(N_TOWER, N_SHARD, ROWS_DEV, N_TOWER, OUT).transpose(3, 1, 0, 2, 4).reshape(N_TOWER, ROWS, OUT)
    tower_grads, stacked, biases = lax.map(tower_backward, (pooled, regroup, down_proj, up_proj, cross_bias, out_proj))
    weight_scale = 1.0 / math.sqrt(ROWS)
    weight_grad = stacked * weight_scale
    returned = tower_grads.reshape(N_TOWER, N_SHARD, N_TOWER, ROWS_DEV, W).transpose(2, 1, 3, 0, 4).reshape(ROWS, N_TOWER * W)
    blocks = returned.reshape(ROWS, FEATURES, EMB)
    inverse = jnp.argsort(assign).astype(jnp.int32)
    feature_grad = jnp.take(blocks, inverse, axis=1).reshape(ROWS, FEATURES * EMB)
    return (feature_grad, weight_grad, biases)
```

```python
import functools
import math

import jax
import jax.numpy as jnp
from jax import lax
from jax.experimental import pallas as pl
from jax.experimental.pallas import tpu as pltpu
from jax.sharding import PartitionSpec as P

MESH = pl.DeviceIdType.MESH
F32 = jnp.float32
BF16 = jnp.bfloat16
NX, NYH, NZ, NYL, NC = 4, 2, 12, 4, 2
TOWERS = NX * NYH
EMB = 128
TILE = 512
LONG, SHORT = 6, 5
NEED = (6, -5, 5, -4, 4, -3, 3, -2, 2, -1, 1, 0)


def dot_nn(a, b):
    return jnp.dot(a, b, preferred_element_type=F32)


def dot_nt(a, b):
    return lax.dot_general(a, b, (((1,), (1,)), ((), ())), preferred_element_type=F32)


def remote(src, dst, send, recv, device):
    return pltpu.make_async_remote_copy(
        src_ref=src, dst_ref=dst, send_sem=send, recv_sem=recv, device_id=device, device_id_type=MESH
    )


def main_kernel(
    scale,
    og_h, x_h, wd_h, wu_h, wo_h, cb_h,
    out_f, out_w, out_b,
    x, wd, wu, wo, cb, go, fac, cr, gc, ggl, gi, part, pair, long_s, long_r, short_s, short_r,
    mine, y_s, y_r, bias, b_pair, b_y, b_z, b_half, b_other,
    in_sem, a1_s, a1_r, a2_s, a2_r, p_s, p_r, l_s, l_r, s_s, s_r, ys_s, ys_r,
    bp_s, bp_r, by_s, by_r, bz_s, bz_r, bf_s, bf_r,
):
    t = lax.axis_index("tower")
    s = lax.axis_index("shard")
    yh, xx = t // NX, t % NX
    z, yl, c = s // (NYL * NC), (s // NC) % NYL, s % NC
    sign = 1 - 2 * c
    rows, width = x.shape
    tiles = width // TILE
    half = width // 2

    def tower_at(i):
        return ((yh + i // NX) % NYH) * NX + (xx + i % NX) % NX

    def shard_at(zz, yy, cc):
        return {"shard": (zz * NYL + yy) * NC + cc}

    order = [i for i in range(NX, TOWERS)] + [i for i in range(1, NX)]
    partner = shard_at(z, yl, 1 - c)
    peers = [{"tower": tower_at(i)} for i in order]
    peers.append(partner)
    peers += [shard_at(z, (yl + j) % NYL, c) for j in range(1, NYL)]
    peers += [shard_at((z + j) % NZ, yl, c) for j in range(1, NZ)]

    barrier = pltpu.get_barrier_semaphore()
    for peer in peers:
        pl.semaphore_signal(barrier, inc=1, device_id=peer, device_id_type=MESH)

    loads = [
        pltpu.make_async_copy(src, dst, in_sem.at[k])
        for k, (src, dst) in enumerate(((x_h, x), (wd_h, wd), (wu_h, wu), (cb_h, cb), (wo_h, wo)))
    ]
    own = pltpu.make_async_copy(
        og_h.at[:, pl.ds(pl.multiple_of(t * 256, 256), 256)], go.at[t], in_sem.at[5]
    )
    for load in loads:
        load.start()
    own.start()
    pl.semaphore_wait(barrier, len(peers))

    first = []
    for i in order:
        dest = tower_at(i)
        first.append(
            remote(
                og_h.at[:, pl.ds(pl.multiple_of(dest * 256, 256), 256)],
                go.at[t], a1_s.at[i], a1_r.at[i], {"tower": dest},
            )
        )
        first[-1].start()

    loads[0].wait()
    loads[1].wait()
    hidden_wide = dot_nn(x[...], wd[...]).astype(BF16)
    hidden_t = hidden_wide.astype(F32).T.astype(BF16)
    loads[2].wait()
    loads[3].wait()

    def forward(k, carry):
        at = pl.ds(pl.multiple_of(k * TILE, TILE), TILE)
        factor = dot_nn(hidden_wide, wu[:, at]) + cb[:, at] + 1.0
        fac[:, at] = factor
        cr[:, at] = (x[:, at].astype(F32) * factor).astype(BF16)
        return carry

    lax.fori_loop(0, tiles, forward, 0)
    loads[4].wait()
    own.wait()
    for copy in first:
        copy.wait_recv()
    grad_out = go[...].reshape(rows, 256)
    grad_out_t = grad_out.astype(F32).T.astype(BF16)

    def crossed_grad(k, total):
        at = pl.ds(pl.multiple_of(k * TILE, TILE), TILE)
        low = dot_nt(grad_out, wo[at, :]).astype(BF16)
        gc[:, at] = low
        gate = low.astype(F32) * x[:, at].astype(F32)
        column = jnp.sum(gate, axis=0, keepdims=True)
        bias[k // (tiles // 2), :, pl.ds(pl.multiple_of((k % (tiles // 2)) * TILE, TILE), TILE)] = column
        gate_low = gate.astype(BF16)
        ggl[:, at] = gate_low
        return total + dot_nt(gate_low, wu[:, at])

    hidden_grad_wide = lax.fori_loop(0, tiles, crossed_grad, jnp.zeros((rows, 256), F32))
    hidden_grad = hidden_grad_wide.astype(BF16)
    hidden_grad_t = hidden_grad.astype(F32).T.astype(BF16)

    def inputs_grad(k, carry):
        at = pl.ds(pl.multiple_of(k * TILE, TILE), TILE)
        value = gc[:, at].astype(F32) * fac[:, at] + dot_nt(hidden_grad, wd[at, :])
        low = value.astype(BF16)
        for a in range(TOWERS):
            for j in range(TILE // EMB):
                gi[a, k * (TILE // EMB) + j] = low[a * 32 : (a + 1) * 32, j * EMB : (j + 1) * EMB]
        return carry

    lax.fori_loop(0, tiles, inputs_grad, 0)
    second = []
    for i in order:
        dest = tower_at(i)
        second.append(remote(gi.at[dest], out_f.at[t], a2_s.at[i], a2_r.at[i], {"tower": dest}))
        second[-1].start()
    keep = pltpu.make_async_copy(gi.at[t], out_f.at[t], in_sem.at[6])
    keep.start()

    bias_pair = remote(bias.at[1 - c], b_pair, bp_s, bp_r, partner)
    bias_pair.start()

    for p, (left, right) in enumerate(((hidden_grad_t, x), (hidden_t, ggl), (grad_out_t, cr))):

        def weights(k, carry):
            at = pl.ds(pl.multiple_of(k * TILE, TILE), TILE)
            value = dot_nn(left, right[:, at])
            for zz in range(4):
                for h in range(2):
                    for cc in range(NC):
                        base = zz * 64 + h * 32 + cc * 8
                        both = jnp.concatenate([value[base : base + 8], value[base + 16 : base + 24]], axis=0)
                        part[cc, p * 4 + zz, h, :, at] = both.astype(BF16)
            return carry

        lax.fori_loop(0, tiles, weights, 0)

    def chunk(offset, direction):
        return (z + direction * offset + NZ) % NZ

    pieces = []
    for k, offset in enumerate(NEED):
        pieces.append(
            remote(part.at[1 - c, chunk(offset, -sign)], pair.at[k], p_s.at[k], p_r.at[k], partner)
        )
        pieces[-1].start()

    ahead = shard_at((z + sign + NZ) % NZ, yl, c)
    behind = shard_at((z - sign + NZ) % NZ, yl, c)
    ring = []

    def local_sum(k, h):
        return part[c, chunk(NEED[k], sign), h].astype(F32) + pair[k, h].astype(F32)

    arms = {
        "long": (long_s, long_r, l_s, l_r, ahead, LONG),
        "short": (short_s, short_r, s_s, s_r, behind, SHORT),
    }
    sent = {}
    bias_y, bias_z = [], []
    for step in range(LONG):
        for name in ("long", "short"):
            if step < arms[name][5]:
                pieces[NEED.index(LONG - step if name == "long" else step - SHORT)].wait_recv()
        for h in range(2):
            for name, (send_ref, recv_ref, send_sem, recv_sem, device, hops) in arms.items():
                if step >= hops:
                    continue
                k = NEED.index(hops - step if name == "long" else step - hops)
                value = local_sum(k, h)
                if step > 0:
                    sent[name, step - 1, h].wait_recv()
                    value = value + recv_ref[step - 1, h].astype(F32)
                send_ref[step, h] = value.astype(BF16)
                copy = remote(
                    send_ref.at[step, h], recv_ref.at[step, h],
                    send_sem.at[step, h], recv_sem.at[step, h], device,
                )
                copy.start()
                sent[name, step, h] = copy
        if step == 0:
            bias_pair.wait_recv()
            b_y[yl] = bias[c] + b_pair[...]
            for j in range(1, NYL):
                copy = remote(b_y.at[yl], b_y.at[yl], by_s.at[j], by_r.at[j], shard_at(z, (yl + j) % NYL, c))
                copy.start()
                bias_y.append(copy)
        if step == 2:
            for copy in bias_y:
                copy.wait_recv()
            b_z[z] = (b_y[0] + b_y[1]) + (b_y[2] + b_y[3])
            for j in range(1, NZ):
                copy = remote(b_z.at[z], b_z.at[z], bz_s.at[j], bz_r.at[j], shard_at((z + j) % NZ, yl, c))
                copy.start()
                bias_z.append(copy)

    pieces[len(NEED) - 1].wait_recv()
    for h in range(2):
        value = local_sum(len(NEED) - 1, h)
        sent["short", SHORT - 1, h].wait_recv()
        value = value + short_r[SHORT - 1, h].astype(F32)
        sent["long", LONG - 1, h].wait_recv()
        value = value + long_r[LONG - 1, h].astype(F32)
        for yy in range(2):
            eight = value[yy * 8 : (yy + 1) * 8]
            mine[h * 2 + yy] = eight
            y_s[h * 2 + yy] = jnp.concatenate([eight[:, :half], eight[:, half:]], axis=0).astype(BF16)
    last = []
    for j in range(1, NYL):
        to = (yl + j) % NYL
        copy = remote(y_s.at[to], y_r.at[j - 1], ys_s.at[j], ys_r.at[j], shard_at(z, to, c))
        copy.start()
        last.append(copy)

    for copy in bias_z:
        copy.wait_recv()
    total = b_z[0]
    for k in range(1, NZ):
        total = total + b_z[k]
    b_half[...] = total
    bias_final = remote(b_half, b_other, bf_s, bf_r, partner)
    bias_final.start()
    out_b[:, pl.ds(pl.multiple_of(c * half, half), half)] = total

    value = mine[yl]
    for copy in last:
        copy.wait_recv()
    for j in range(NYL - 1):
        got = y_r[j].astype(F32)
        value = value + jnp.concatenate([got[:8], got[8:]], axis=1)
    out_w[...] = value * scale

    bias_final.wait_recv()
    out_b[:, pl.ds(pl.multiple_of((1 - c) * half, half), half)] = b_other[...]

    keep.wait()
    for copy in second:
        copy.wait_recv()
    for copy in first + second + pieces + list(sent.values()) + bias_y + bias_z + last + [bias_pair, bias_final]:
        copy.wait_send()


def place_kernel(assign_ref, f_ref, w_ref, b_ref, out_f, out_w, out_b):
    for k in range(f_ref.shape[0]):
        out_f[:, pl.ds(pl.multiple_of(assign_ref[k] * EMB, EMB), EMB)] = f_ref[k]
    out_w[...] = w_ref[...]
    out_b[...] = b_ref[...]


def body(out_grad, pooled, down_proj, up_proj, cross_bias, out_proj, assign):
    rows, width = pooled.shape[1:]
    any_space = pl.BlockSpec(memory_space=pl.ANY)
    vmem = pl.BlockSpec(memory_space=pltpu.VMEM)
    scale = 1.0 / math.sqrt(rows * lax.axis_size("shard"))
    dma = pltpu.SemaphoreType.DMA
    quarter = width // 2
    moved, weights, bias = pl.pallas_call(
        functools.partial(main_kernel, scale),
        out_shape=(
            jax.ShapeDtypeStruct((TOWERS, width // EMB, 32, EMB), BF16),
            jax.ShapeDtypeStruct((8, width), F32),
            jax.ShapeDtypeStruct((1, width), F32),
        ),
        in_specs=[any_space] * 6,
        out_specs=(any_space, vmem, vmem),
        scratch_shapes=[
            pltpu.VMEM((rows, width), BF16),
            pltpu.VMEM((width, 256), BF16),
            pltpu.VMEM((256, width), BF16),
            pltpu.VMEM((width, 256), BF16),
            pltpu.VMEM((1, width), F32),
            pltpu.VMEM((TOWERS, 32, 256), BF16),
            pltpu.VMEM((rows, width), F32),
            pltpu.VMEM((rows, width), BF16),
            pltpu.VMEM((rows, width), BF16),
            pltpu.VMEM((rows, width), BF16),
            pltpu.VMEM((TOWERS, width // EMB, 32, EMB), BF16),
            pltpu.VMEM((NC, NZ, 2, 16, width), BF16),
            pltpu.VMEM((NZ, 2, 16, width), BF16),
            pltpu.VMEM((LONG, 2, 16, width), BF16),
            pltpu.VMEM((LONG, 2, 16, width), BF16),
            pltpu.VMEM((SHORT, 2, 16, width), BF16),
            pltpu.VMEM((SHORT, 2, 16, width), BF16),
            pltpu.VMEM((NYL, 8, width), F32),
            pltpu.VMEM((NYL, 16, quarter), BF16),
            pltpu.VMEM((NYL - 1, 16, quarter), BF16),
            pltpu.VMEM((2, 1, quarter), F32),
            pltpu.VMEM((1, quarter), F32),
            pltpu.VMEM((NYL, 1, quarter), F32),
            pltpu.VMEM((NZ, 1, quarter), F32),
            pltpu.VMEM((1, quarter), F32),
            pltpu.VMEM((1, quarter), F32),
            dma((7,)),
            dma((TOWERS,)), dma((TOWERS,)), dma((TOWERS,)), dma((TOWERS,)),
            dma((NZ,)), dma((NZ,)),
            dma((LONG, 2)), dma((LONG, 2)), dma((SHORT, 2)), dma((SHORT, 2)),
            dma((NYL,)), dma((NYL,)),
            dma, dma, dma((NYL,)), dma((NYL,)), dma((NZ,)), dma((NZ,)), dma, dma,
        ],
        compiler_params=pltpu.CompilerParams(
            collective_id=0, has_side_effects=True, vmem_limit_bytes=65000 * 1024
        ),
        name="tower_backward",
    )(out_grad, pooled[0], down_proj[0], up_proj[0], out_proj[0], cross_bias)
    feature_grad, weight_grad, bias_grad = pl.pallas_call(
        place_kernel,
        out_shape=(
            jax.ShapeDtypeStruct((32, TOWERS * width), BF16),
            jax.ShapeDtypeStruct((8, width), F32),
            jax.ShapeDtypeStruct((1, width), F32),
        ),
        in_specs=[pl.BlockSpec(memory_space=pltpu.SMEM), vmem, vmem, vmem],
        out_specs=(vmem, vmem, vmem),
        name="place_columns",
    )(assign, moved.reshape(TOWERS * (width // EMB), 32, EMB), weights, bias)
    return (feature_grad, weight_grad[None], bias_grad)


def solution(mesh):
    placed = (
        P(("tower", "shard"), None),
        P("tower", "shard", None),
        P("tower", None, None),
        P("tower", None, None),
        P("tower", None),
        P("tower", None, None),
        P(),
    )
    return jax.shard_map(
        body,
        mesh=mesh,
        in_specs=placed,
        out_specs=(P(("tower", "shard"), None), P("tower", "shard", None), P("tower", None)),
        check_vma=False,
    )
```

```python
import functools
import math

import jax
import jax.numpy as jnp
from jax import lax
from jax.experimental import pallas as pl
from jax.experimental.pallas import tpu as pltpu
from jax.sharding import PartitionSpec as P

MESH = pl.DeviceIdType.MESH
F32 = jnp.float32
BF16 = jnp.bfloat16
NX, NYH, NZ, NYL, NC = 4, 2, 12, 4, 2
TOWERS = NX * NYH
EMB = 128
TILE = 512
LONG, SHORT = 6, 5
SUBS = ((0, 0), (0, 1), (1, 0), (1, 1))
NEED = (6, -5, 5, -4, 4, -3, 3, -2, 2, -1, 1, 0)


def dot_nn(a, b):
    return jnp.dot(a, b, preferred_element_type=F32)


def dot_nt(a, b):
    return lax.dot_general(a, b, (((1,), (1,)), ((), ())), preferred_element_type=F32)


def remote(src, dst, send, recv, device):
    return pltpu.make_async_remote_copy(
        src_ref=src, dst_ref=dst, send_sem=send, recv_sem=recv, device_id=device, device_id_type=MESH
    )


def main_kernel(
    scale,
    og_h, x_h, wd_h, wu_h, wo_h, cb_h,
    out_f, out_w, out_b,
    x, wd, wu, wo, cb, go, fac, cr, gc, ggl, gi, part, pair, long_s, long_r, short_s, short_r,
    og, mine, y_s, y_r, bias, b_pair, b_y, b_z, b_half, b_other,
    in_sem, og_sem, a1_s, a1_r, a2_s, a2_r, p_s, p_r, l_s, l_r, s_s, s_r, ys_s, ys_r,
    bp_s, bp_r, by_s, by_r, bz_s, bz_r, bf_s, bf_r,
):
    t = lax.axis_index("tower")
    s = lax.axis_index("shard")
    yh, xx = t // NX, t % NX
    z, yl, c = s // (NYL * NC), (s // NC) % NYL, s % NC
    sign = 1 - 2 * c
    rows, width = x.shape
    tiles = width // TILE
    half = width // 2

    def tower_at(i):
        return ((yh + i // NX) % NYH) * NX + (xx + i % NX) % NX

    def shard_at(zz, yy, cc):
        return {"shard": (zz * NYL + yy) * NC + cc}

    order = [i for i in range(NX, TOWERS)] + [i for i in range(1, NX)]
    partner = shard_at(z, yl, 1 - c)
    peers = [{"tower": tower_at(i)} for i in order]
    peers.append(partner)
    peers += [shard_at(z, (yl + j) % NYL, c) for j in range(1, NYL)]
    peers += [shard_at((z + j) % NZ, yl, c) for j in range(1, NZ)]

    barrier = pltpu.get_barrier_semaphore()
    for peer in peers:
        pl.semaphore_signal(barrier, inc=1, device_id=peer, device_id_type=MESH)

    loads = [
        pltpu.make_async_copy(src, dst, in_sem.at[k])
        for k, (src, dst) in enumerate(((x_h, x), (wd_h, wd), (wu_h, wu), (cb_h, cb), (wo_h, wo)))
    ]
    own = pltpu.make_async_copy(
        og_h.at[:, pl.ds(pl.multiple_of(t * 256, 256), 256)], go.at[t], in_sem.at[5]
    )
    stage = []
    for i in order:
        dest = tower_at(i)
        stage.append(
            pltpu.make_async_copy(og_h.at[:, pl.ds(pl.multiple_of(dest * 256, 256), 256)], og.at[dest], og_sem.at[i])
        )
        stage[-1].start()
    own.start()
    for load in loads:
        load.start()
    for copy in stage:
        copy.wait()
    pl.semaphore_wait(barrier, len(peers))

    first = []
    for i in order:
        dest = tower_at(i)
        first.append(remote(og.at[dest], go.at[t], a1_s.at[i], a1_r.at[i], {"tower": dest}))
        first[-1].start()

    loads[0].wait()
    loads[1].wait()
    hidden_wide = dot_nn(x[...], wd[...]).astype(BF16)
    hidden_t = hidden_wide.astype(F32).T.astype(BF16)
    loads[2].wait()
    loads[3].wait()

    spans = [pl.ds(k * TILE, TILE) for k in range(tiles)]
    for at in spans:
        factor = dot_nn(hidden_wide, wu[:, at]) + cb[:, at] + 1.0
        fac[:, at] = factor
        cr[:, at] = (x[:, at].astype(F32) * factor).astype(BF16)
    loads[4].wait()
    own.wait()
    for copy in first:
        copy.wait_recv()
    grad_out = go[...].reshape(rows, 256)

    def weights(p, left, right):
        for k, at in enumerate(spans):
            q, low = k * TILE // half, k * TILE % half
            value = dot_nn(left, right[:, at])
            for zz in range(4):
                for h in range(2):
                    for cc in range(NC):
                        base = zz * 64 + h * 32 + cc * 8
                        both = jnp.concatenate([value[base : base + 8], value[base + 16 : base + 24]], axis=0)
                        part[cc, p * 4 + zz, h, q, :, low : low + TILE] = both.astype(BF16)

    hidden_grad_wide = jnp.zeros((rows, 256), F32)
    for k, at in enumerate(spans):
        low = dot_nt(grad_out, wo[at, :]).astype(BF16)
        gc[:, at] = low
        gate = low.astype(F32) * x[:, at].astype(F32)
        bias[k * TILE // half, :, k * TILE % half : k * TILE % half + TILE] = jnp.sum(gate, axis=0, keepdims=True)
        gate_low = gate.astype(BF16)
        ggl[:, at] = gate_low
        hidden_grad_wide = hidden_grad_wide + dot_nt(gate_low, wu[:, at])
    hidden_grad = hidden_grad_wide.astype(BF16)
    bias_pair = remote(bias.at[1 - c], b_pair, bp_s, bp_r, partner)
    bias_pair.start()
    weights(2, grad_out.astype(F32).T.astype(BF16), cr)
    weights(1, hidden_t, ggl)
    weights(0, hidden_grad.astype(F32).T.astype(BF16), x)

    def chunk(offset, direction):
        return (z + direction * offset + NZ) % NZ

    pieces = []
    for k, offset in enumerate(NEED):
        pieces.append(
            remote(part.at[1 - c, chunk(offset, -sign)], pair.at[k], p_s.at[k], p_r.at[k], partner)
        )
        pieces[-1].start()

    for k, at in enumerate(spans):
        value = gc[:, at].astype(F32) * fac[:, at] + dot_nt(hidden_grad, wd[at, :])
        low = value.astype(BF16)
        for a in range(TOWERS):
            for j in range(TILE // EMB):
                gi[a, k * (TILE // EMB) + j] = low[a * 32 : (a + 1) * 32, j * EMB : (j + 1) * EMB]
    second = []
    for i in order:
        dest = tower_at(i)
        second.append(remote(gi.at[dest], out_f.at[t], a2_s.at[i], a2_r.at[i], {"tower": dest}))
        second[-1].start()
    keep = pltpu.make_async_copy(gi.at[t], out_f.at[t], in_sem.at[6])
    keep.start()

    ahead = shard_at((z + sign + NZ) % NZ, yl, c)
    behind = shard_at((z - sign + NZ) % NZ, yl, c)

    def local_sum(k, h, q):
        return part[c, chunk(NEED[k], sign), h, q].astype(F32) + pair[k, h, q].astype(F32)

    arms = {
        "long": (long_s, long_r, l_s, l_r, ahead, LONG),
        "short": (short_s, short_r, s_s, s_r, behind, SHORT),
    }
    sent = {}
    bias_y, bias_z = [], []
    for step in range(LONG):
        for name in ("long", "short"):
            if step < arms[name][5]:
                pieces[NEED.index(LONG - step if name == "long" else step - SHORT)].wait_recv()
        for h, q in SUBS:
            for name, (send_ref, recv_ref, send_sem, recv_sem, device, hops) in arms.items():
                if step >= hops:
                    continue
                value = local_sum(NEED.index(hops - step if name == "long" else step - hops), h, q)
                if step > 0:
                    sent[name, step - 1, h, q].wait_recv()
                    value = value + recv_ref[step - 1, h, q].astype(F32)
                send_ref[step, h, q] = value.astype(BF16)
                copy = remote(
                    send_ref.at[step, h, q], recv_ref.at[step, h, q],
                    send_sem.at[step, h * 2 + q], recv_sem.at[step, h * 2 + q], device,
                )
                copy.start()
                sent[name, step, h, q] = copy
        if step == 0:
            bias_pair.wait_recv()
            b_z[z] = bias[c] + b_pair[...]
            for j in range(1, NZ):
                copy = remote(b_z.at[z], b_z.at[z], bz_s.at[j], bz_r.at[j], shard_at((z + j) % NZ, yl, c))
                copy.start()
                bias_z.append(copy)
        if step == 3:
            for copy in bias_z:
                copy.wait_recv()
            column = b_z[0]
            for k in range(1, NZ):
                column = column + b_z[k]
            b_y[yl] = column
            for j in range(1, NYL):
                copy = remote(b_y.at[yl], b_y.at[yl], by_s.at[j], by_r.at[j], shard_at(z, (yl + j) % NYL, c))
                copy.start()
                bias_y.append(copy)

    pieces[len(NEED) - 1].wait_recv()
    for h in range(2):
        halves = []
        for q in range(2):
            value = local_sum(len(NEED) - 1, h, q)
            sent["short", SHORT - 1, h, q].wait_recv()
            value = value + short_r[SHORT - 1, h, q].astype(F32)
            sent["long", LONG - 1, h, q].wait_recv()
            halves.append(value + long_r[LONG - 1, h, q].astype(F32))
        for yy in range(2):
            eight = [value[yy * 8 : (yy + 1) * 8] for value in halves]
            for q in range(2):
                mine[h * 2 + yy, :, q * half : (q + 1) * half] = eight[q]
            y_s[h * 2 + yy] = jnp.concatenate(eight, axis=0).astype(BF16)
    last = []
    for j in range(1, NYL):
        to = (yl + j) % NYL
        copy = remote(y_s.at[to], y_r.at[j - 1], ys_s.at[j], ys_r.at[j], shard_at(z, to, c))
        copy.start()
        last.append(copy)

    for copy in bias_y:
        copy.wait_recv()
    total = (b_y[0] + b_y[1]) + (b_y[2] + b_y[3])
    b_half[...] = total
    bias_final = remote(b_half, b_other, bf_s, bf_r, partner)
    bias_final.start()
    out_b[:, pl.ds(pl.multiple_of(c * half, half), half)] = total

    value = mine[yl]
    for copy in last:
        copy.wait_recv()
    for j in range(NYL - 1):
        got = y_r[j].astype(F32)
        value = value + jnp.concatenate([got[:8], got[8:]], axis=1)
    out_w[...] = value * scale

    bias_final.wait_recv()
    out_b[:, pl.ds(pl.multiple_of((1 - c) * half, half), half)] = b_other[...]

    keep.wait()
    for copy in second:
        copy.wait_recv()
    for copy in first + second + pieces + list(sent.values()) + bias_y + bias_z + last + [bias_pair, bias_final]:
        copy.wait_send()


def place_kernel(assign_ref, f_ref, w_ref, b_ref, out_f, out_w, out_b, slot_of, held, placed, in_sem, out_sem):
    slots = f_ref.shape[0]
    each = slots // TOWERS
    loads = []
    for n in range(TOWERS):
        loads.append(
            pltpu.make_async_copy(f_ref.at[pl.ds(n * each, each)], held.at[pl.ds(n * each, each)], in_sem.at[n])
        )
        loads[-1].start()
    out_w[...] = w_ref[...]
    out_b[...] = b_ref[...]

    def invert(k, carry):
        slot_of[assign_ref[k]] = k
        return carry

    lax.fori_loop(0, slots, invert, 0, unroll=8)
    for load in loads:
        load.wait()
    stores = []
    for n in range(TOWERS):
        for feature in range(n * each, (n + 1) * each):
            placed[:, feature * EMB : (feature + 1) * EMB] = held[slot_of[feature]]
        at = pl.ds(n * each * EMB, each * EMB)
        stores.append(pltpu.make_async_copy(placed.at[:, at], out_f.at[:, at], out_sem.at[n]))
        stores[-1].start()
    for store in stores:
        store.wait()


def body(out_grad, pooled, down_proj, up_proj, cross_bias, out_proj, assign):
    rows, width = pooled.shape[1:]
    any_space = pl.BlockSpec(memory_space=pl.ANY)
    vmem = pl.BlockSpec(memory_space=pltpu.VMEM)
    scale = 1.0 / math.sqrt(rows * lax.axis_size("shard"))
    dma = pltpu.SemaphoreType.DMA
    half = width // 2
    moved, weights, bias = pl.pallas_call(
        functools.partial(main_kernel, scale),
        out_shape=(
            jax.ShapeDtypeStruct((TOWERS, width // EMB, 32, EMB), BF16),
            jax.ShapeDtypeStruct((8, width), F32),
            jax.ShapeDtypeStruct((1, width), F32),
        ),
        in_specs=[any_space] * 6,
        out_specs=(any_space, vmem, vmem),
        scratch_shapes=[
            pltpu.VMEM((rows, width), BF16),
            pltpu.VMEM((width, 256), BF16),
            pltpu.VMEM((256, width), BF16),
            pltpu.VMEM((width, 256), BF16),
            pltpu.VMEM((1, width), F32),
            pltpu.VMEM((TOWERS, 32, 256), BF16),
            pltpu.VMEM((rows, width), F32),
            pltpu.VMEM((rows, width), BF16),
            pltpu.VMEM((rows, width), BF16),
            pltpu.VMEM((rows, width), BF16),
            pltpu.VMEM((TOWERS, width // EMB, 32, EMB), BF16),
            pltpu.VMEM((NC, NZ, 2, 2, 16, half), BF16),
            pltpu.VMEM((NZ, 2, 2, 16, half), BF16),
            pltpu.VMEM((LONG, 2, 2, 16, half), BF16),
            pltpu.VMEM((LONG, 2, 2, 16, half), BF16),
            pltpu.VMEM((SHORT, 2, 2, 16, half), BF16),
            pltpu.VMEM((SHORT, 2, 2, 16, half), BF16),
            pltpu.VMEM((TOWERS, 32, 256), BF16),
            pltpu.VMEM((NYL, 8, width), F32),
            pltpu.VMEM((NYL, 16, half), BF16),
            pltpu.VMEM((NYL - 1, 16, half), BF16),
            pltpu.VMEM((2, 1, half), F32),
            pltpu.VMEM((1, half), F32),
            pltpu.VMEM((NYL, 1, half), F32),
            pltpu.VMEM((NZ, 1, half), F32),
            pltpu.VMEM((1, half), F32),
            pltpu.VMEM((1, half), F32),
            dma((7,)),
            dma((TOWERS,)),
            dma((TOWERS,)), dma((TOWERS,)), dma((TOWERS,)), dma((TOWERS,)),
            dma((NZ,)), dma((NZ,)),
            dma((LONG, 4)), dma((LONG, 4)), dma((SHORT, 4)), dma((SHORT, 4)),
            dma((NYL,)), dma((NYL,)),
            dma, dma, dma((NYL,)), dma((NYL,)), dma((NZ,)), dma((NZ,)), dma, dma,
        ],
        compiler_params=pltpu.CompilerParams(
            collective_id=0, has_side_effects=True, vmem_limit_bytes=65000 * 1024
        ),
        name="tower_backward",
    )(out_grad, pooled[0], down_proj[0], up_proj[0], out_proj[0], cross_bias)
    feature_grad, weight_grad, bias_grad = pl.pallas_call(
        place_kernel,
        out_shape=(
            jax.ShapeDtypeStruct((32, TOWERS * width), BF16),
            jax.ShapeDtypeStruct((8, width), F32),
            jax.ShapeDtypeStruct((1, width), F32),
        ),
        in_specs=[pl.BlockSpec(memory_space=pltpu.SMEM), any_space, vmem, vmem],
        out_specs=(any_space, vmem, vmem),
        scratch_shapes=[
            pltpu.SMEM((TOWERS * (width // EMB),), jnp.int32),
            pltpu.VMEM((TOWERS * (width // EMB), 32, EMB), BF16),
            pltpu.VMEM((32, TOWERS * width), BF16),
            dma((TOWERS,)),
            dma((TOWERS,)),
        ],
        compiler_params=pltpu.CompilerParams(vmem_limit_bytes=65000 * 1024),
        name="place_columns",
    )(assign, moved.reshape(TOWERS * (width // EMB), 32, EMB), weights, bias)
    return (feature_grad, weight_grad[None], bias_grad)


def solution(mesh):
    placed = (
        P(("tower", "shard"), None),
        P("tower", "shard", None),
        P("tower", None, None),
        P("tower", None, None),
        P("tower", None),
        P("tower", None, None),
        P(),
    )
    return jax.shard_map(
        body,
        mesh=mesh,
        in_specs=placed,
        out_specs=(P(("tower", "shard"), None), P("tower", "shard", None), P("tower", None)),
        check_vma=False,
    )
```

```python
import functools
import math

import jax
import jax.numpy as jnp
from jax import lax
from jax.experimental import pallas as pl
from jax.experimental.pallas import tpu as pltpu
from jax.sharding import PartitionSpec as P

MESH = pl.DeviceIdType.MESH
F32 = jnp.float32
BF16 = jnp.bfloat16
NX, NYH, NZ, NYL, NC = 4, 2, 12, 4, 2
TOWERS = NX * NYH
EMB = 128
TILE = 512
LONG, SHORT = 6, 5
SUBS = ((0, 0), (0, 1), (1, 0), (1, 1))
NEED = (6, -5, 5, -4, 4, -3, 3, -2, 2, -1, 1, 0)


def dot_nn(a, b):
    return jnp.dot(a, b, preferred_element_type=F32)


def dot_nt(a, b):
    return lax.dot_general(a, b, (((1,), (1,)), ((), ())), preferred_element_type=F32)


def remote(src, dst, send, recv, device):
    return pltpu.make_async_remote_copy(
        src_ref=src, dst_ref=dst, send_sem=send, recv_sem=recv, device_id=device, device_id_type=MESH
    )


def main_kernel(
    scale,
    og_h, x_h, wd_h, wu_h, wo_h, cb_h,
    out_f, out_w, out_b,
    x, wd, wu, wo, cb, go, fac, cr, gc, ggl, gi, part, pair, long_s, long_r, short_s, short_r,
    og, mine, y_s, y_r, bias, b_pair, b_y, b_z, b_half, b_other,
    in_sem, og_sem, a1_s, a1_r, a2_s, a2_r, p_s, p_r, l_s, l_r, s_s, s_r, ys_s, ys_r,
    bp_s, bp_r, by_s, by_r, bz_s, bz_r, bf_s, bf_r,
):
    t = lax.axis_index("tower")
    s = lax.axis_index("shard")
    yh, xx = t // NX, t % NX
    z, yl, c = s // (NYL * NC), (s // NC) % NYL, s % NC
    sign = 1 - 2 * c
    rows, width = x.shape
    tiles = width // TILE
    half = width // 2

    def tower_at(i):
        return ((yh + i // NX) % NYH) * NX + (xx + i % NX) % NX

    def shard_at(zz, yy, cc):
        return {"shard": (zz * NYL + yy) * NC + cc}

    order = (6, 5, 7, 4, 2, 1, 3)
    partner = shard_at(z, yl, 1 - c)
    peers = [{"tower": tower_at(i)} for i in order]
    peers.append(partner)
    peers += [shard_at(z, (yl + j) % NYL, c) for j in range(1, NYL)]
    peers += [shard_at((z + j) % NZ, yl, c) for j in range(1, NZ)]

    barrier = pltpu.get_barrier_semaphore()
    for peer in peers:
        pl.semaphore_signal(barrier, inc=1, device_id=peer, device_id_type=MESH)

    loads = [
        pltpu.make_async_copy(src, dst, in_sem.at[k])
        for k, (src, dst) in enumerate(((x_h, x), (wd_h, wd), (wu_h, wu), (cb_h, cb), (wo_h, wo)))
    ]
    own = pltpu.make_async_copy(
        og_h.at[:, pl.ds(pl.multiple_of(t * 256, 256), 256)], go.at[t], in_sem.at[5]
    )
    stage = []
    for i in order:
        dest = tower_at(i)
        stage.append(
            pltpu.make_async_copy(og_h.at[:, pl.ds(pl.multiple_of(dest * 256, 256), 256)], og.at[dest], og_sem.at[i])
        )
        stage[-1].start()
    own.start()
    for load in loads:
        load.start()
    for copy in stage:
        copy.wait()
    pl.semaphore_wait(barrier, len(peers))

    first = []
    for i in order:
        dest = tower_at(i)
        first.append(remote(og.at[dest], go.at[t], a1_s.at[i], a1_r.at[i], {"tower": dest}))
        first[-1].start()

    loads[0].wait()
    loads[1].wait()
    hidden_wide = dot_nn(x[...], wd[...]).astype(BF16)
    hidden_t = hidden_wide.astype(F32).T.astype(BF16)
    loads[2].wait()
    loads[3].wait()

    spans = [pl.ds(k * TILE, TILE) for k in range(tiles)]
    for at in spans:
        factor = dot_nn(hidden_wide, wu[:, at]) + cb[:, at] + 1.0
        fac[:, at] = factor
        cr[:, at] = (x[:, at].astype(F32) * factor).astype(BF16)
    loads[4].wait()
    own.wait()
    for copy in first:
        copy.wait_recv()
    grad_out = go[...].reshape(rows, 256)

    def weights(p, left, right):
        for k, at in enumerate(spans):
            q, low = k * TILE // half, k * TILE % half
            value = dot_nn(left, right[:, at])
            for zz in range(4):
                for h in range(2):
                    for cc in range(NC):
                        base = zz * 64 + h * 32 + cc * 8
                        both = jnp.concatenate([value[base : base + 8], value[base + 16 : base + 24]], axis=0)
                        part[cc, p * 4 + zz, h, q, :, low : low + TILE] = both.astype(BF16)

    hidden_grad_wide = jnp.zeros((rows, 256), F32)
    for k, at in enumerate(spans):
        low = dot_nt(grad_out, wo[at, :]).astype(BF16)
        gc[:, at] = low
        gate = low.astype(F32) * x[:, at].astype(F32)
        bias[k * TILE // half, :, k * TILE % half : k * TILE % half + TILE] = jnp.sum(gate, axis=0, keepdims=True)
        gate_low = gate.astype(BF16)
        ggl[:, at] = gate_low
        hidden_grad_wide = hidden_grad_wide + dot_nt(gate_low, wu[:, at])
    hidden_grad = hidden_grad_wide.astype(BF16)
    bias_pair = remote(bias.at[1 - c], b_pair, bp_s, bp_r, partner)
    bias_pair.start()
    weights(2, grad_out.astype(F32).T.astype(BF16), cr)
    weights(1, hidden_t, ggl)
    weights(0, hidden_grad.astype(F32).T.astype(BF16), x)

    def chunk(offset, direction):
        return (z + direction * offset + NZ) % NZ

    pieces = []
    for k, offset in enumerate(NEED):
        pieces.append(
            remote(part.at[1 - c, chunk(offset, -sign)], pair.at[k], p_s.at[k], p_r.at[k], partner)
        )
        pieces[-1].start()

    for k, at in enumerate(spans):
        value = gc[:, at].astype(F32) * fac[:, at] + dot_nt(hidden_grad, wd[at, :])
        low = value.astype(BF16)
        for a in range(TOWERS):
            for j in range(TILE // EMB):
                gi[a, k * (TILE // EMB) + j] = low[a * 32 : (a + 1) * 32, j * EMB : (j + 1) * EMB]
    second = []
    for i in order:
        dest = tower_at(i)
        second.append(remote(gi.at[dest], out_f.at[t], a2_s.at[i], a2_r.at[i], {"tower": dest}))
        second[-1].start()
    keep = pltpu.make_async_copy(gi.at[t], out_f.at[t], in_sem.at[6])
    keep.start()

    ahead = shard_at((z + sign + NZ) % NZ, yl, c)
    behind = shard_at((z - sign + NZ) % NZ, yl, c)

    def local_sum(k, h, q):
        return part[c, chunk(NEED[k], sign), h, q].astype(F32) + pair[k, h, q].astype(F32)

    arms = {
        "long": (long_s, long_r, l_s, l_r, ahead, LONG),
        "short": (short_s, short_r, s_s, s_r, behind, SHORT),
    }
    sent = {}
    bias_y, bias_z = [], []
    for step in range(LONG):
        for name in ("long", "short"):
            if step < arms[name][5]:
                pieces[NEED.index(LONG - step if name == "long" else step - SHORT)].wait_recv()
        for h, q in SUBS:
            for name, (send_ref, recv_ref, send_sem, recv_sem, device, hops) in arms.items():
                if step >= hops:
                    continue
                value = local_sum(NEED.index(hops - step if name == "long" else step - hops), h, q)
                if step > 0:
                    sent[name, step - 1, h, q].wait_recv()
                    value = value + recv_ref[step - 1, h, q].astype(F32)
                send_ref[step, h, q] = value.astype(BF16)
                copy = remote(
                    send_ref.at[step, h, q], recv_ref.at[step, h, q],
                    send_sem.at[step, h * 2 + q], recv_sem.at[step, h * 2 + q], device,
                )
                copy.start()
                sent[name, step, h, q] = copy
        if step == 0:
            bias_pair.wait_recv()
            b_z[z] = bias[c] + b_pair[...]
            for j in range(1, NZ):
                copy = remote(b_z.at[z], b_z.at[z], bz_s.at[j], bz_r.at[j], shard_at((z + j) % NZ, yl, c))
                copy.start()
                bias_z.append(copy)
        if step == 3:
            for copy in bias_z:
                copy.wait_recv()
            column = b_z[0]
            for k in range(1, NZ):
                column = column + b_z[k]
            b_y[yl] = column
            for j in range(1, NYL):
                copy = remote(b_y.at[yl], b_y.at[yl], by_s.at[j], by_r.at[j], shard_at(z, (yl + j) % NYL, c))
                copy.start()
                bias_y.append(copy)

    pieces[len(NEED) - 1].wait_recv()
    for h in range(2):
        halves = []
        for q in range(2):
            value = local_sum(len(NEED) - 1, h, q)
            sent["short", SHORT - 1, h, q].wait_recv()
            value = value + short_r[SHORT - 1, h, q].astype(F32)
            sent["long", LONG - 1, h, q].wait_recv()
            halves.append(value + long_r[LONG - 1, h, q].astype(F32))
        for yy in range(2):
            eight = [value[yy * 8 : (yy + 1) * 8] for value in halves]
            for q in range(2):
                mine[h * 2 + yy, :, q * half : (q + 1) * half] = eight[q]
            y_s[h * 2 + yy] = jnp.concatenate(eight, axis=0).astype(BF16)
    last = []
    for j in range(1, NYL):
        to = (yl + j) % NYL
        copy = remote(y_s.at[to], y_r.at[j - 1], ys_s.at[j], ys_r.at[j], shard_at(z, to, c))
        copy.start()
        last.append(copy)

    for copy in bias_y:
        copy.wait_recv()
    total = (b_y[0] + b_y[1]) + (b_y[2] + b_y[3])
    b_half[...] = total
    bias_final = remote(b_half, b_other, bf_s, bf_r, partner)
    bias_final.start()
    out_b[:, pl.ds(pl.multiple_of(c * half, half), half)] = total

    value = mine[yl]
    for copy in last:
        copy.wait_recv()
    for j in range(NYL - 1):
        got = y_r[j].astype(F32)
        value = value + jnp.concatenate([got[:8], got[8:]], axis=1)
    out_w[...] = value * scale

    bias_final.wait_recv()
    out_b[:, pl.ds(pl.multiple_of((1 - c) * half, half), half)] = b_other[...]

    keep.wait()
    for copy in second:
        copy.wait_recv()
    for copy in first + second + pieces + list(sent.values()) + bias_y + bias_z + last + [bias_pair, bias_final]:
        copy.wait_send()


def place_kernel(assign_ref, f_ref, w_ref, b_ref, out_f, out_w, out_b):
    for k in range(f_ref.shape[0]):
        out_f[:, pl.ds(pl.multiple_of(assign_ref[k] * EMB, EMB), EMB)] = f_ref[k]
    out_w[...] = w_ref[...]
    out_b[...] = b_ref[...]


def body(out_grad, pooled, down_proj, up_proj, cross_bias, out_proj, assign):
    rows, width = pooled.shape[1:]
    any_space = pl.BlockSpec(memory_space=pl.ANY)
    vmem = pl.BlockSpec(memory_space=pltpu.VMEM)
    scale = 1.0 / math.sqrt(rows * lax.axis_size("shard"))
    dma = pltpu.SemaphoreType.DMA
    half = width // 2
    moved, weights, bias = pl.pallas_call(
        functools.partial(main_kernel, scale),
        out_shape=(
            jax.ShapeDtypeStruct((TOWERS, width // EMB, 32, EMB), BF16),
            jax.ShapeDtypeStruct((8, width), F32),
            jax.ShapeDtypeStruct((1, width), F32),
        ),
        in_specs=[any_space] * 6,
        out_specs=(any_space, vmem, vmem),
        scratch_shapes=[
            pltpu.VMEM((rows, width), BF16),
            pltpu.VMEM((width, 256), BF16),
            pltpu.VMEM((256, width), BF16),
            pltpu.VMEM((width, 256), BF16),
            pltpu.VMEM((1, width), F32),
            pltpu.VMEM((TOWERS, 32, 256), BF16),
            pltpu.VMEM((rows, width), F32),
            pltpu.VMEM((rows, width), BF16),
            pltpu.VMEM((rows, width), BF16),
            pltpu.VMEM((rows, width), BF16),
            pltpu.VMEM((TOWERS, width // EMB, 32, EMB), BF16),
            pltpu.VMEM((NC, NZ, 2, 2, 16, half), BF16),
            pltpu.VMEM((NZ, 2, 2, 16, half), BF16),
            pltpu.VMEM((LONG, 2, 2, 16, half), BF16),
            pltpu.VMEM((LONG, 2, 2, 16, half), BF16),
            pltpu.VMEM((SHORT, 2, 2, 16, half), BF16),
            pltpu.VMEM((SHORT, 2, 2, 16, half), BF16),
            pltpu.VMEM((TOWERS, 32, 256), BF16),
            pltpu.VMEM((NYL, 8, width), F32),
            pltpu.VMEM((NYL, 16, half), BF16),
            pltpu.VMEM((NYL - 1, 16, half), BF16),
            pltpu.VMEM((2, 1, half), F32),
            pltpu.VMEM((1, half), F32),
            pltpu.VMEM((NYL, 1, half), F32),
            pltpu.VMEM((NZ, 1, half), F32),
            pltpu.VMEM((1, half), F32),
            pltpu.VMEM((1, half), F32),
            dma((7,)),
            dma((TOWERS,)),
            dma((TOWERS,)), dma((TOWERS,)), dma((TOWERS,)), dma((TOWERS,)),
            dma((NZ,)), dma((NZ,)),
            dma((LONG, 4)), dma((LONG, 4)), dma((SHORT, 4)), dma((SHORT, 4)),
            dma((NYL,)), dma((NYL,)),
            dma, dma, dma((NYL,)), dma((NYL,)), dma((NZ,)), dma((NZ,)), dma, dma,
        ],
        compiler_params=pltpu.CompilerParams(
            collective_id=0, has_side_effects=True, vmem_limit_bytes=65000 * 1024
        ),
        name="tower_backward",
    )(out_grad, pooled[0], down_proj[0], up_proj[0], out_proj[0], cross_bias)
    feature_grad, weight_grad, bias_grad = pl.pallas_call(
        place_kernel,
        out_shape=(
            jax.ShapeDtypeStruct((32, TOWERS * width), BF16),
            jax.ShapeDtypeStruct((8, width), F32),
            jax.ShapeDtypeStruct((1, width), F32),
        ),
        in_specs=[pl.BlockSpec(memory_space=pltpu.SMEM), vmem, vmem, vmem],
        out_specs=(vmem, vmem, vmem),
        name="place_columns",
    )(assign, moved.reshape(TOWERS * (width // EMB), 32, EMB), weights, bias)
    return (feature_grad, weight_grad[None], bias_grad)


def solution(mesh):
    placed = (
        P(("tower", "shard"), None),
        P("tower", "shard", None),
        P("tower", None, None),
        P("tower", None, None),
        P("tower", None),
        P("tower", None, None),
        P(),
    )
    return jax.shard_map(
        body,
        mesh=mesh,
        in_specs=placed,
        out_specs=(P(("tower", "shard"), None), P("tower", "shard", None), P("tower", None)),
        check_vma=False,
    )
```

```python
import functools
import math

import jax
import jax.numpy as jnp
from jax import lax
from jax.experimental import pallas as pl
from jax.experimental.pallas import tpu as pltpu
from jax.sharding import PartitionSpec as P

MESH = pl.DeviceIdType.MESH
F32 = jnp.float32
BF16 = jnp.bfloat16
NX, NYH, NZ, NYL, NC = 4, 2, 12, 4, 2
TOWERS = NX * NYH
EMB = 128
TILE = 512
LONG, SHORT = 6, 5
NEED = (6, -5, 5, -4, 4, -3, 3, -2, 2, -1, 1, 0)


def dot_nn(a, b):
    return jnp.dot(a, b, preferred_element_type=F32)


def dot_nt(a, b):
    return lax.dot_general(a, b, (((1,), (1,)), ((), ())), preferred_element_type=F32)


def remote(src, dst, send, recv, device):
    return pltpu.make_async_remote_copy(
        src_ref=src, dst_ref=dst, send_sem=send, recv_sem=recv, device_id=device, device_id_type=MESH
    )


def main_kernel(
    scale,
    og_h, x_h, wd_h, wu_h, wo_h, cb_h,
    out_f, out_w, out_b,
    x, wd, wu, wo, cb, go, fac, cr, gc, ggl, gi, part, pair, long_s, long_r, short_s, short_r,
    og, f_s, f_r, mine, y_s, y_r, bias, b_pair, b_y, b_z, b_half, b_other,
    in_sem, og_sem, a1_s, a1_r, a2_s, a2_r, p_s, p_r, l_s, l_r, s_s, s_r, ys_s, ys_r, fs_s, fs_r,
    bp_s, bp_r, by_s, by_r, bz_s, bz_r, bf_s, bf_r,
):
    t = lax.axis_index("tower")
    s = lax.axis_index("shard")
    yh, xx = t // NX, t % NX
    z, yl, c = s // (NYL * NC), (s // NC) % NYL, s % NC
    sign = 1 - 2 * c
    rows, width = x.shape
    tiles = width // TILE
    half = width // 2

    def tower_at(i):
        return ((yh + i // NX) % NYH) * NX + (xx + i % NX) % NX

    def shard_at(zz, yy, cc):
        return {"shard": (zz * NYL + yy) * NC + cc}

    order = (6, 5, 7, 4, 2, 1, 3)
    partner = shard_at(z, yl, 1 - c)
    peers = [{"tower": tower_at(i)} for i in order]
    peers.append(partner)
    peers += [shard_at(z, (yl + j) % NYL, c) for j in range(1, NYL)]
    peers += [shard_at((z + j) % NZ, yl, c) for j in range(1, NZ)]
    peers += [shard_at((z + d) % NZ, (yl + j) % NYL, c) for d in (1, NZ - 1) for j in range(1, NYL)]

    barrier = pltpu.get_barrier_semaphore()
    for peer in peers:
        pl.semaphore_signal(barrier, inc=1, device_id=peer, device_id_type=MESH)

    loads = [
        pltpu.make_async_copy(src, dst, in_sem.at[k])
        for k, (src, dst) in enumerate(((x_h, x), (wd_h, wd), (wu_h, wu), (cb_h, cb), (wo_h, wo)))
    ]
    own = pltpu.make_async_copy(
        og_h.at[:, pl.ds(pl.multiple_of(t * 256, 256), 256)], go.at[t], in_sem.at[5]
    )
    stage = []
    for i in order:
        dest = tower_at(i)
        stage.append(
            pltpu.make_async_copy(og_h.at[:, pl.ds(pl.multiple_of(dest * 256, 256), 256)], og.at[dest], og_sem.at[i])
        )
        stage[-1].start()
    own.start()
    for load in loads:
        load.start()
    for copy in stage:
        copy.wait()
    pl.semaphore_wait(barrier, len(peers))

    first = []
    for i in order:
        dest = tower_at(i)
        first.append(remote(og.at[dest], go.at[t], a1_s.at[i], a1_r.at[i], {"tower": dest}))
        first[-1].start()

    loads[0].wait()
    loads[1].wait()
    hidden_wide = dot_nn(x[...], wd[...]).astype(BF16)
    hidden_t = hidden_wide.astype(F32).T.astype(BF16)
    loads[2].wait()
    loads[3].wait()

    spans = [pl.ds(k * TILE, TILE) for k in range(tiles)]
    for at in spans:
        factor = dot_nn(hidden_wide, wu[:, at]) + cb[:, at] + 1.0
        fac[:, at] = factor
        cr[:, at] = (x[:, at].astype(F32) * factor).astype(BF16)
    loads[4].wait()
    own.wait()
    for copy in first:
        copy.wait_recv()
    grad_out = go[...].reshape(rows, 256)

    def weights(p, left, right):
        for k, at in enumerate(spans):
            q, low = k * TILE // half, k * TILE % half
            value = dot_nn(left, right[:, at])
            for zz in range(4):
                for h in range(2):
                    for cc in range(NC):
                        base = zz * 64 + h * 32 + cc * 8
                        both = jnp.concatenate([value[base : base + 8], value[base + 16 : base + 24]], axis=0)
                        part[cc, p * 4 + zz, h, q, :, low : low + TILE] = both.astype(BF16)

    hidden_grad_wide = jnp.zeros((rows, 256), F32)
    for k, at in enumerate(spans):
        low = dot_nt(grad_out, wo[at, :]).astype(BF16)
        gc[:, at] = low
        gate = low.astype(F32) * x[:, at].astype(F32)
        bias[k * TILE // half, :, k * TILE % half : k * TILE % half + TILE] = jnp.sum(gate, axis=0, keepdims=True)
        gate_low = gate.astype(BF16)
        ggl[:, at] = gate_low
        hidden_grad_wide = hidden_grad_wide + dot_nt(gate_low, wu[:, at])
    hidden_grad = hidden_grad_wide.astype(BF16)
    bias_pair = remote(bias.at[1 - c], b_pair, bp_s, bp_r, partner)
    bias_pair.start()
    weights(2, grad_out.astype(F32).T.astype(BF16), cr)
    weights(1, hidden_t, ggl)
    weights(0, hidden_grad.astype(F32).T.astype(BF16), x)

    def chunk(offset, direction):
        return (z + direction * offset + NZ) % NZ

    pieces = []
    for k, offset in enumerate(NEED):
        pieces.append(
            remote(part.at[1 - c, chunk(offset, -sign)], pair.at[k], p_s.at[k], p_r.at[k], partner)
        )
        pieces[-1].start()

    for k, at in enumerate(spans):
        value = gc[:, at].astype(F32) * fac[:, at] + dot_nt(hidden_grad, wd[at, :])
        low = value.astype(BF16)
        for a in range(TOWERS):
            for j in range(TILE // EMB):
                gi[a, k * (TILE // EMB) + j] = low[a * 32 : (a + 1) * 32, j * EMB : (j + 1) * EMB]
    second = []
    for i in order:
        dest = tower_at(i)
        second.append(remote(gi.at[dest], out_f.at[t], a2_s.at[i], a2_r.at[i], {"tower": dest}))
        second[-1].start()
    keep = pltpu.make_async_copy(gi.at[t], out_f.at[t], in_sem.at[6])
    keep.start()

    ahead, behind = (z + sign + NZ) % NZ, (z - sign + NZ) % NZ

    def local_sum(k, h, q):
        return part[c, chunk(NEED[k], sign), h, q].astype(F32) + pair[k, h, q].astype(F32)

    arms = {
        "long": (long_s, long_r, l_s, l_r, ahead, LONG),
        "short": (short_s, short_r, s_s, s_r, behind, SHORT),
    }
    sent = {}
    bias_y, bias_z, last = [], [], []

    def eights(values, yy):
        return jnp.concatenate([value[yy * 8 : (yy + 1) * 8] for value in values], axis=0).astype(BF16)

    def whole(got):
        wide = got.astype(F32)
        return jnp.concatenate([wide[:8], wide[8:]], axis=1)

    for step in range(LONG):
        for name in ("long", "short"):
            if step < arms[name][5]:
                pieces[NEED.index(LONG - step if name == "long" else step - SHORT)].wait_recv()
        for h in range(2):
            for arm, (name, (send_ref, recv_ref, send_sem, recv_sem, to, hops)) in enumerate(arms.items()):
                if step >= hops:
                    continue
                values = []
                for q in range(2):
                    value = local_sum(NEED.index(hops - step if name == "long" else step - hops), h, q)
                    if step > 0:
                        sent[name, step - 1, h, q].wait_recv()
                        value = value + recv_ref[step - 1, h, q].astype(F32)
                    values.append(value)
                    if step < hops - 1:
                        send_ref[step, h, q] = value.astype(BF16)
                        copy = remote(
                            send_ref.at[step, h, q], recv_ref.at[step, h, q],
                            send_sem.at[step, h * 2 + q], recv_sem.at[step, h * 2 + q], shard_at(to, yl, c),
                        )
                        copy.start()
                        sent[name, step, h, q] = copy
                if step == hops - 1:
                    for yy in range(2):
                        row = h * 2 + yy
                        f_s[arm, row] = eights(values, yy)
                        copy = remote(
                            f_s.at[arm, row], f_r.at[arm, yl],
                            fs_s.at[arm, row], fs_r.at[arm, yl], shard_at(to, row, c),
                        )
                        copy.start()
                        sent[name, step, row] = copy
        if step == 1:
            pieces[len(NEED) - 1].wait_recv()
            for h in range(2):
                values = [local_sum(len(NEED) - 1, h, q) for q in range(2)]
                for yy in range(2):
                    y_s[h * 2 + yy] = eights(values, yy)
                    for q in range(2):
                        mine[h * 2 + yy, :, q * half : (q + 1) * half] = values[q][yy * 8 : (yy + 1) * 8]
            for j in range(1, NYL):
                to = (yl + j) % NYL
                copy = remote(y_s.at[to], y_r.at[j - 1], ys_s.at[j], ys_r.at[j], shard_at(z, to, c))
                copy.start()
                last.append(copy)
        if step == 0:
            bias_pair.wait_recv()
            b_z[z] = bias[c] + b_pair[...]
            for j in range(1, NZ):
                copy = remote(b_z.at[z], b_z.at[z], bz_s.at[j], bz_r.at[j], shard_at((z + j) % NZ, yl, c))
                copy.start()
                bias_z.append(copy)
        if step == 3:
            for copy in bias_z:
                copy.wait_recv()
            column = b_z[0]
            for k in range(1, NZ):
                column = column + b_z[k]
            b_y[yl] = column
            for j in range(1, NYL):
                copy = remote(b_y.at[yl], b_y.at[yl], by_s.at[j], by_r.at[j], shard_at(z, (yl + j) % NYL, c))
                copy.start()
                bias_y.append(copy)

    value = mine[yl]
    for copy in last:
        copy.wait_recv()
    for j in range(NYL - 1):
        value = value + whole(y_r[j])
    for k in range(NYL):
        remote(f_s.at[1, k], f_r.at[1, k], fs_s.at[1, k], fs_r.at[1, k], partner).wait_recv()
        value = value + whole(f_r[1, k])
    for copy in bias_y:
        copy.wait_recv()
    total = (b_y[0] + b_y[1]) + (b_y[2] + b_y[3])
    b_half[...] = total
    bias_final = remote(b_half, b_other, bf_s, bf_r, partner)
    bias_final.start()
    out_b[:, pl.ds(pl.multiple_of(c * half, half), half)] = total

    for k in range(NYL):
        remote(f_s.at[0, k], f_r.at[0, k], fs_s.at[0, k], fs_r.at[0, k], partner).wait_recv()
        value = value + whole(f_r[0, k])
    out_w[...] = value * scale

    bias_final.wait_recv()
    out_b[:, pl.ds(pl.multiple_of((1 - c) * half, half), half)] = b_other[...]

    keep.wait()
    for copy in second:
        copy.wait_recv()
    for copy in first + second + pieces + list(sent.values()) + bias_y + bias_z + last + [bias_pair, bias_final]:
        copy.wait_send()


def place_kernel(assign_ref, f_ref, w_ref, b_ref, out_f, out_w, out_b):
    for k in range(f_ref.shape[0]):
        out_f[:, pl.ds(pl.multiple_of(assign_ref[k] * EMB, EMB), EMB)] = f_ref[k]
    out_w[...] = w_ref[...]
    out_b[...] = b_ref[...]


def body(out_grad, pooled, down_proj, up_proj, cross_bias, out_proj, assign):
    rows, width = pooled.shape[1:]
    any_space = pl.BlockSpec(memory_space=pl.ANY)
    vmem = pl.BlockSpec(memory_space=pltpu.VMEM)
    scale = 1.0 / math.sqrt(rows * lax.axis_size("shard"))
    dma = pltpu.SemaphoreType.DMA
    half = width // 2
    moved, weights, bias = pl.pallas_call(
        functools.partial(main_kernel, scale),
        out_shape=(
            jax.ShapeDtypeStruct((TOWERS, width // EMB, 32, EMB), BF16),
            jax.ShapeDtypeStruct((8, width), F32),
            jax.ShapeDtypeStruct((1, width), F32),
        ),
        in_specs=[any_space] * 6,
        out_specs=(any_space, vmem, vmem),
        scratch_shapes=[
            pltpu.VMEM((rows, width), BF16),
            pltpu.VMEM((width, 256), BF16),
            pltpu.VMEM((256, width), BF16),
            pltpu.VMEM((width, 256), BF16),
            pltpu.VMEM((1, width), F32),
            pltpu.VMEM((TOWERS, 32, 256), BF16),
            pltpu.VMEM((rows, width), F32),
            pltpu.VMEM((rows, width), BF16),
            pltpu.VMEM((rows, width), BF16),
            pltpu.VMEM((rows, width), BF16),
            pltpu.VMEM((TOWERS, width // EMB, 32, EMB), BF16),
            pltpu.VMEM((NC, NZ, 2, 2, 16, half), BF16),
            pltpu.VMEM((NZ, 2, 2, 16, half), BF16),
            pltpu.VMEM((LONG, 2, 2, 16, half), BF16),
            pltpu.VMEM((LONG, 2, 2, 16, half), BF16),
            pltpu.VMEM((SHORT, 2, 2, 16, half), BF16),
            pltpu.VMEM((SHORT, 2, 2, 16, half), BF16),
            pltpu.VMEM((TOWERS, 32, 256), BF16),
            pltpu.VMEM((2, NYL, 16, half), BF16),
            pltpu.VMEM((2, NYL, 16, half), BF16),
            pltpu.VMEM((NYL, 8, width), F32),
            pltpu.VMEM((NYL, 16, half), BF16),
            pltpu.VMEM((NYL - 1, 16, half), BF16),
            pltpu.VMEM((2, 1, half), F32),
            pltpu.VMEM((1, half), F32),
            pltpu.VMEM((NYL, 1, half), F32),
            pltpu.VMEM((NZ, 1, half), F32),
            pltpu.VMEM((1, half), F32),
            pltpu.VMEM((1, half), F32),
            dma((7,)),
            dma((TOWERS,)),
            dma((TOWERS,)), dma((TOWERS,)), dma((TOWERS,)), dma((TOWERS,)),
            dma((NZ,)), dma((NZ,)),
            dma((LONG, 4)), dma((LONG, 4)), dma((SHORT, 4)), dma((SHORT, 4)),
            dma((NYL,)), dma((NYL,)), dma((2, NYL)), dma((2, NYL)),
            dma, dma, dma((NYL,)), dma((NYL,)), dma((NZ,)), dma((NZ,)), dma, dma,
        ],
        compiler_params=pltpu.CompilerParams(
            collective_id=0, has_side_effects=True, vmem_limit_bytes=65000 * 1024
        ),
        name="tower_backward",
    )(out_grad, pooled[0], down_proj[0], up_proj[0], out_proj[0], cross_bias)
    feature_grad, weight_grad, bias_grad = pl.pallas_call(
        place_kernel,
        out_shape=(
            jax.ShapeDtypeStruct((32, TOWERS * width), BF16),
            jax.ShapeDtypeStruct((8, width), F32),
            jax.ShapeDtypeStruct((1, width), F32),
        ),
        in_specs=[pl.BlockSpec(memory_space=pltpu.SMEM), vmem, vmem, vmem],
        out_specs=(vmem, vmem, vmem),
        name="place_columns",
    )(assign, moved.reshape(TOWERS * (width // EMB), 32, EMB), weights, bias)
    return (feature_grad, weight_grad[None], bias_grad)


def solution(mesh):
    placed = (
        P(("tower", "shard"), None),
        P("tower", "shard", None),
        P("tower", None, None),
        P("tower", None, None),
        P("tower", None),
        P("tower", None, None),
        P(),
    )
    return jax.shard_map(
        body,
        mesh=mesh,
        in_specs=placed,
        out_specs=(P(("tower", "shard"), None), P("tower", "shard", None), P("tower", None)),
        check_vma=False,
    )
```

```python
import functools
import math

import jax
import jax.numpy as jnp
from jax import lax
from jax.experimental import pallas as pl
from jax.experimental.pallas import tpu as pltpu
from jax.sharding import PartitionSpec as P

MESH = pl.DeviceIdType.MESH
F32 = jnp.float32
BF16 = jnp.bfloat16
NX, NYH, NZ, NYL, NC = 4, 2, 12, 4, 2
TOWERS = NX * NYH
EMB = 128
TILE = 512
LONG, SHORT = 6, 5
SUBS = ((0, 0), (0, 1), (1, 0), (1, 1))
NEED = (6, -5, 5, -4, 4, -3, 3, -2, 2, -1, 1, 0)


def dot_nn(a, b):
    return jnp.dot(a, b, preferred_element_type=F32)


def dot_nt(a, b):
    return lax.dot_general(a, b, (((1,), (1,)), ((), ())), preferred_element_type=F32)


def remote(src, dst, send, recv, device):
    return pltpu.make_async_remote_copy(
        src_ref=src, dst_ref=dst, send_sem=send, recv_sem=recv, device_id=device, device_id_type=MESH
    )


def main_kernel(
    scale,
    og_h, x_h, wd_h, wu_h, wo_h, cb_h,
    out_f, out_w, out_b,
    x, wd, wu, wo, cb, go, fac, cr, gc, ggl, gi, part, pair, long_s, long_r, short_s, short_r,
    og, mine, y_s, y_r, bias, b_pair, b_y, b_z, b_half, b_other,
    in_sem, og_sem, a1_s, a1_r, a2_s, a2_r, p_s, p_r, l_s, l_r, s_s, s_r, ys_s, ys_r,
    bp_s, bp_r, by_s, by_r, bz_s, bz_r, bf_s, bf_r,
):
    t = lax.axis_index("tower")
    s = lax.axis_index("shard")
    yh, xx = t // NX, t % NX
    z, yl, c = s // (NYL * NC), (s // NC) % NYL, s % NC
    sign = 1 - 2 * c
    rows, width = x.shape
    tiles = width // TILE
    half = width // 2

    def tower_at(i):
        return ((yh + i // NX) % NYH) * NX + (xx + i % NX) % NX

    def shard_at(zz, yy, cc):
        return {"shard": (zz * NYL + yy) * NC + cc}

    order = (6, 5, 7, 4, 2, 1, 3)
    partner = shard_at(z, yl, 1 - c)
    peers = [{"tower": tower_at(i)} for i in order]
    peers.append(partner)
    peers += [shard_at(z, (yl + j) % NYL, c) for j in range(1, NYL)]
    peers += [shard_at((z + j) % NZ, yl, c) for j in range(1, NZ)]

    barrier = pltpu.get_barrier_semaphore()
    for peer in peers:
        pl.semaphore_signal(barrier, inc=1, device_id=peer, device_id_type=MESH)

    loads = [
        pltpu.make_async_copy(src, dst, in_sem.at[k])
        for k, (src, dst) in enumerate(((x_h, x), (wd_h, wd), (wu_h, wu), (cb_h, cb), (wo_h, wo)))
    ]
    own = pltpu.make_async_copy(
        og_h.at[:, pl.ds(pl.multiple_of(t * 256, 256), 256)], go.at[t], in_sem.at[5]
    )
    stage = []
    for i in order:
        dest = tower_at(i)
        stage.append(
            pltpu.make_async_copy(og_h.at[:, pl.ds(pl.multiple_of(dest * 256, 256), 256)], og.at[dest], og_sem.at[i])
        )
        stage[-1].start()
    own.start()
    for load in loads:
        load.start()
    for copy in stage:
        copy.wait()
    pl.semaphore_wait(barrier, len(peers))

    first = []
    for i in order:
        dest = tower_at(i)
        first.append(remote(og.at[dest], go.at[t], a1_s.at[i], a1_r.at[i], {"tower": dest}))
        first[-1].start()

    loads[0].wait()
    loads[1].wait()
    hidden_wide = dot_nn(x[...], wd[...]).astype(BF16)
    hidden_t = hidden_wide.astype(F32).T.astype(BF16)
    loads[2].wait()
    loads[3].wait()

    spans = [pl.ds(k * TILE, TILE) for k in range(tiles)]
    for at in spans:
        factor = dot_nn(hidden_wide, wu[:, at]) + cb[:, at] + 1.0
        fac[:, at] = factor
        cr[:, at] = (x[:, at].astype(F32) * factor).astype(BF16)
    loads[4].wait()
    own.wait()
    for copy in first:
        copy.wait_recv()
    grad_out = go[...].reshape(rows, 256)

    def weights(p, left, right):
        for k, at in enumerate(spans):
            q, low = k * TILE // half, k * TILE % half
            value = dot_nn(left, right[:, at])
            for zz in range(4):
                for h in range(2):
                    for cc in range(NC):
                        base = zz * 64 + h * 32 + cc * 8
                        both = jnp.concatenate([value[base : base + 8], value[base + 16 : base + 24]], axis=0)
                        part[cc, p * 4 + zz, h, q, :, low : low + TILE] = both.astype(BF16)

    hidden_grad_wide = jnp.zeros((rows, 256), F32)
    for k, at in enumerate(spans):
        low = dot_nt(grad_out, wo[at, :]).astype(BF16)
        gc[:, at] = low
        gate = low.astype(F32) * x[:, at].astype(F32)
        bias[k * TILE // half, :, k * TILE % half : k * TILE % half + TILE] = jnp.sum(gate, axis=0, keepdims=True)
        gate_low = gate.astype(BF16)
        ggl[:, at] = gate_low
        hidden_grad_wide = hidden_grad_wide + dot_nt(gate_low, wu[:, at])
    hidden_grad = hidden_grad_wide.astype(BF16)
    bias_pair = remote(bias.at[1 - c], b_pair, bp_s, bp_r, partner)
    bias_pair.start()
    weights(2, grad_out.astype(F32).T.astype(BF16), cr)
    weights(1, hidden_t, ggl)
    weights(0, hidden_grad.astype(F32).T.astype(BF16), x)

    def chunk(offset, direction):
        return (z + direction * offset + NZ) % NZ

    pieces = []
    for k, offset in enumerate(NEED):
        pieces.append(
            remote(part.at[1 - c, chunk(offset, -sign)], pair.at[k], p_s.at[k], p_r.at[k], partner)
        )
        pieces[-1].start()

    for k, at in enumerate(spans):
        value = gc[:, at].astype(F32) * fac[:, at] + dot_nt(hidden_grad, wd[at, :])
        low = value.astype(BF16)
        for a in range(TOWERS):
            for j in range(TILE // EMB):
                gi[a, k * (TILE // EMB) + j] = low[a * 32 : (a + 1) * 32, j * EMB : (j + 1) * EMB]
    second = []
    for i in order:
        dest = tower_at(i)
        second.append(remote(gi.at[dest], out_f.at[t], a2_s.at[i], a2_r.at[i], {"tower": dest}))
        second[-1].start()
    keep = pltpu.make_async_copy(gi.at[t], out_f.at[t], in_sem.at[6])
    keep.start()

    ahead = shard_at((z + sign + NZ) % NZ, yl, c)
    behind = shard_at((z - sign + NZ) % NZ, yl, c)

    def local_sum(k, h, q):
        return part[c, chunk(NEED[k], sign), h, q].astype(F32) + pair[k, h, q].astype(F32)

    arms = {
        "long": (long_s, long_r, l_s, l_r, ahead, LONG),
        "short": (short_s, short_r, s_s, s_r, behind, SHORT),
    }
    sent = {}
    bias_y, bias_z = [], []
    ahead2 = shard_at((z + 2 * sign + NZ) % NZ, yl, c)
    for step in range(SHORT):
        for name in ("long", "short"):
            if step < arms[name][5]:
                pieces[NEED.index(LONG - step if name == "long" else step - SHORT)].wait_recv()
        for h, q in SUBS:
            for name, (send_ref, recv_ref, send_sem, recv_sem, device, hops) in arms.items():
                if step >= hops:
                    continue
                value = local_sum(NEED.index(hops - step if name == "long" else step - hops), h, q)
                if step > 0:
                    sent[name, step - 1, h, q].wait_recv()
                    value = value + recv_ref[step - 1, h, q].astype(F32)
                send_ref[step, h, q] = value.astype(BF16)
                to = ahead2 if name == "long" and step == SHORT - 1 else device
                copy = remote(
                    send_ref.at[step, h, q], recv_ref.at[step, h, q],
                    send_sem.at[step, h * 2 + q], recv_sem.at[step, h * 2 + q], to,
                )
                copy.start()
                sent[name, step, h, q] = copy
        if step == 1:
            near = NEED.index(1)
            pieces[near].wait_recv()
            for h, q in SUBS:
                long_s[LONG - 1, h, q] = local_sum(near, h, q).astype(BF16)
                copy = remote(
                    long_s.at[LONG - 1, h, q], long_r.at[LONG - 1, h, q],
                    l_s.at[LONG - 1, h * 2 + q], l_r.at[LONG - 1, h * 2 + q], ahead,
                )
                copy.start()
                sent["near", 0, h, q] = copy
        if step == 0:
            bias_pair.wait_recv()
            b_z[z] = bias[c] + b_pair[...]
            for j in range(1, NZ):
                copy = remote(b_z.at[z], b_z.at[z], bz_s.at[j], bz_r.at[j], shard_at((z + j) % NZ, yl, c))
                copy.start()
                bias_z.append(copy)
        if step == 3:
            for copy in bias_z:
                copy.wait_recv()
            column = b_z[0]
            for k in range(1, NZ):
                column = column + b_z[k]
            b_y[yl] = column
            for j in range(1, NYL):
                copy = remote(b_y.at[yl], b_y.at[yl], by_s.at[j], by_r.at[j], shard_at(z, (yl + j) % NYL, c))
                copy.start()
                bias_y.append(copy)

    pieces[len(NEED) - 1].wait_recv()
    for h in range(2):
        halves = []
        for q in range(2):
            value = local_sum(len(NEED) - 1, h, q)
            sent["short", SHORT - 1, h, q].wait_recv()
            value = value + short_r[SHORT - 1, h, q].astype(F32)
            sent["near", 0, h, q].wait_recv()
            value = value + long_r[LONG - 1, h, q].astype(F32)
            sent["long", SHORT - 1, h, q].wait_recv()
            halves.append(value + long_r[SHORT - 1, h, q].astype(F32))
        for yy in range(2):
            eight = [value[yy * 8 : (yy + 1) * 8] for value in halves]
            for q in range(2):
                mine[h * 2 + yy, :, q * half : (q + 1) * half] = eight[q]
            y_s[h * 2 + yy] = jnp.concatenate(eight, axis=0).astype(BF16)
    last = []
    for j in range(1, NYL):
        to = (yl + j) % NYL
        copy = remote(y_s.at[to], y_r.at[j - 1], ys_s.at[j], ys_r.at[j], shard_at(z, to, c))
        copy.start()
        last.append(copy)

    for copy in bias_y:
        copy.wait_recv()
    total = (b_y[0] + b_y[1]) + (b_y[2] + b_y[3])
    b_half[...] = total
    bias_final = remote(b_half, b_other, bf_s, bf_r, partner)
    bias_final.start()
    out_b[:, pl.ds(pl.multiple_of(c * half, half), half)] = total

    value = mine[yl]
    for copy in last:
        copy.wait_recv()
    for j in range(NYL - 1):
        got = y_r[j].astype(F32)
        value = value + jnp.concatenate([got[:8], got[8:]], axis=1)
    out_w[...] = value * scale

    bias_final.wait_recv()
    out_b[:, pl.ds(pl.multiple_of((1 - c) * half, half), half)] = b_other[...]

    keep.wait()
    for copy in second:
        copy.wait_recv()
    for copy in first + second + pieces + list(sent.values()) + bias_y + bias_z + last + [bias_pair, bias_final]:
        copy.wait_send()


def place_kernel(assign_ref, f_ref, w_ref, b_ref, out_f, out_w, out_b):
    for k in range(f_ref.shape[0]):
        out_f[:, pl.ds(pl.multiple_of(assign_ref[k] * EMB, EMB), EMB)] = f_ref[k]
    out_w[...] = w_ref[...]
    out_b[...] = b_ref[...]


def body(out_grad, pooled, down_proj, up_proj, cross_bias, out_proj, assign):
    rows, width = pooled.shape[1:]
    any_space = pl.BlockSpec(memory_space=pl.ANY)
    vmem = pl.BlockSpec(memory_space=pltpu.VMEM)
    scale = 1.0 / math.sqrt(rows * lax.axis_size("shard"))
    dma = pltpu.SemaphoreType.DMA
    half = width // 2
    moved, weights, bias = pl.pallas_call(
        functools.partial(main_kernel, scale),
        out_shape=(
            jax.ShapeDtypeStruct((TOWERS, width // EMB, 32, EMB), BF16),
            jax.ShapeDtypeStruct((8, width), F32),
            jax.ShapeDtypeStruct((1, width), F32),
        ),
        in_specs=[any_space] * 6,
        out_specs=(any_space, vmem, vmem),
        scratch_shapes=[
            pltpu.VMEM((rows, width), BF16),
            pltpu.VMEM((width, 256), BF16),
            pltpu.VMEM((256, width), BF16),
            pltpu.VMEM((width, 256), BF16),
            pltpu.VMEM((1, width), F32),
            pltpu.VMEM((TOWERS, 32, 256), BF16),
            pltpu.VMEM((rows, width), F32),
            pltpu.VMEM((rows, width), BF16),
            pltpu.VMEM((rows, width), BF16),
            pltpu.VMEM((rows, width), BF16),
            pltpu.VMEM((TOWERS, width // EMB, 32, EMB), BF16),
            pltpu.VMEM((NC, NZ, 2, 2, 16, half), BF16),
            pltpu.VMEM((NZ, 2, 2, 16, half), BF16),
            pltpu.VMEM((LONG, 2, 2, 16, half), BF16),
            pltpu.VMEM((LONG, 2, 2, 16, half), BF16),
            pltpu.VMEM((SHORT, 2, 2, 16, half), BF16),
            pltpu.VMEM((SHORT, 2, 2, 16, half), BF16),
            pltpu.VMEM((TOWERS, 32, 256), BF16),
            pltpu.VMEM((NYL, 8, width), F32),
            pltpu.VMEM((NYL, 16, half), BF16),
            pltpu.VMEM((NYL - 1, 16, half), BF16),
            pltpu.VMEM((2, 1, half), F32),
            pltpu.VMEM((1, half), F32),
            pltpu.VMEM((NYL, 1, half), F32),
            pltpu.VMEM((NZ, 1, half), F32),
            pltpu.VMEM((1, half), F32),
            pltpu.VMEM((1, half), F32),
            dma((7,)),
            dma((TOWERS,)),
            dma((TOWERS,)), dma((TOWERS,)), dma((TOWERS,)), dma((TOWERS,)),
            dma((NZ,)), dma((NZ,)),
            dma((LONG, 4)), dma((LONG, 4)), dma((SHORT, 4)), dma((SHORT, 4)),
            dma((NYL,)), dma((NYL,)),
            dma, dma, dma((NYL,)), dma((NYL,)), dma((NZ,)), dma((NZ,)), dma, dma,
        ],
        compiler_params=pltpu.CompilerParams(
            collective_id=0, has_side_effects=True, vmem_limit_bytes=65000 * 1024
        ),
        name="tower_backward",
    )(out_grad, pooled[0], down_proj[0], up_proj[0], out_proj[0], cross_bias)
    feature_grad, weight_grad, bias_grad = pl.pallas_call(
        place_kernel,
        out_shape=(
            jax.ShapeDtypeStruct((32, TOWERS * width), BF16),
            jax.ShapeDtypeStruct((8, width), F32),
            jax.ShapeDtypeStruct((1, width), F32),
        ),
        in_specs=[pl.BlockSpec(memory_space=pltpu.SMEM), vmem, vmem, vmem],
        out_specs=(vmem, vmem, vmem),
        name="place_columns",
    )(assign, moved.reshape(TOWERS * (width // EMB), 32, EMB), weights, bias)
    return (feature_grad, weight_grad[None], bias_grad)


def solution(mesh):
    placed = (
        P(("tower", "shard"), None),
        P("tower", "shard", None),
        P("tower", None, None),
        P("tower", None, None),
        P("tower", None),
        P("tower", None, None),
        P(),
    )
    return jax.shard_map(
        body,
        mesh=mesh,
        in_specs=placed,
        out_specs=(P(("tower", "shard"), None), P("tower", "shard", None), P("tower", None)),
        check_vma=False,
    )
```

```python
import functools
import math

import jax
import jax.numpy as jnp
from jax import lax
from jax.experimental import pallas as pl
from jax.experimental.pallas import tpu as pltpu
from jax.sharding import PartitionSpec as P

MESH = pl.DeviceIdType.MESH
F32 = jnp.float32
BF16 = jnp.bfloat16
NX, NYH, NZ, NYL, NC = 4, 2, 12, 4, 2
TOWERS = NX * NYH
EMB = 128
TILE = 512
LONG, SHORT = 6, 5
SUBS = ((0, 0), (0, 1), (1, 0), (1, 1))
NEED = (6, -5, 5, -4, 4, -3, 3, -2, 2, -1, 1, 0)


def dot_nn(a, b):
    return jnp.dot(a, b, preferred_element_type=F32)


def dot_nt(a, b):
    return lax.dot_general(a, b, (((1,), (1,)), ((), ())), preferred_element_type=F32)


def remote(src, dst, send, recv, device):
    return pltpu.make_async_remote_copy(
        src_ref=src, dst_ref=dst, send_sem=send, recv_sem=recv, device_id=device, device_id_type=MESH
    )


def main_kernel(
    scale,
    og_h, x_h, wd_h, wu_h, wo_h, cb_h,
    out_f, out_w, out_b,
    x, wd, wu, wo, cb, go, fac, cr, gc, ggl, gi, part, pair, long_s, long_r, short_s, short_r,
    og, mine, y_s, y_r, bias, b_pair, b_y, b_z, b_half, b_other,
    in_sem, og_sem, a1_s, a1_r, a2_s, a2_r, p_s, p_r, l_s, l_r, s_s, s_r, ys_s, ys_r,
    bp_s, bp_r, by_s, by_r, bz_s, bz_r, bf_s, bf_r,
):
    t = lax.axis_index("tower")
    s = lax.axis_index("shard")
    yh, xx = t // NX, t % NX
    z, yl, c = s // (NYL * NC), (s // NC) % NYL, s % NC
    sign = 1 - 2 * c
    rows, width = x.shape
    tiles = width // TILE
    half = width // 2

    def tower_at(i):
        return ((yh + i // NX) % NYH) * NX + (xx + i % NX) % NX

    def shard_at(zz, yy, cc):
        return {"shard": (zz * NYL + yy) * NC + cc}

    order = (6, 5, 7, 4, 2, 1, 3)
    partner = shard_at(z, yl, 1 - c)
    peers = [{"tower": tower_at(i)} for i in order]
    peers.append(partner)
    peers += [shard_at(z, (yl + j) % NYL, c) for j in range(1, NYL)]
    peers += [shard_at((z + j) % NZ, yl, c) for j in range(1, NZ)]

    barrier = pltpu.get_barrier_semaphore()
    for peer in peers:
        pl.semaphore_signal(barrier, inc=1, device_id=peer, device_id_type=MESH)

    loads = [
        pltpu.make_async_copy(src, dst, in_sem.at[k])
        for k, (src, dst) in enumerate(((x_h, x), (wd_h, wd), (wu_h, wu), (cb_h, cb), (wo_h, wo)))
    ]
    own = pltpu.make_async_copy(
        og_h.at[:, pl.ds(pl.multiple_of(t * 256, 256), 256)], go.at[t], in_sem.at[5]
    )
    stage = []
    for i in order:
        dest = tower_at(i)
        stage.append(
            pltpu.make_async_copy(og_h.at[:, pl.ds(pl.multiple_of(dest * 256, 256), 256)], og.at[dest], og_sem.at[i])
        )
        stage[-1].start()
    own.start()
    for load in loads:
        load.start()
    for copy in stage:
        copy.wait()
    pl.semaphore_wait(barrier, len(peers))

    first = []
    for i in order:
        dest = tower_at(i)
        first.append(remote(og.at[dest], go.at[t], a1_s.at[i], a1_r.at[i], {"tower": dest}))
        first[-1].start()

    loads[0].wait()
    loads[1].wait()
    hidden_wide = dot_nn(x[...], wd[...]).astype(BF16)
    hidden_t = hidden_wide.astype(F32).T.astype(BF16)
    loads[2].wait()
    loads[3].wait()

    spans = [pl.ds(k * TILE, TILE) for k in range(tiles)]
    for at in spans:
        factor = dot_nn(hidden_wide, wu[:, at]) + cb[:, at] + 1.0
        fac[:, at] = factor
        cr[:, at] = (x[:, at].astype(F32) * factor).astype(BF16)
    loads[4].wait()
    own.wait()
    for copy in first:
        copy.wait_recv()
    grad_out = go[...].reshape(rows, 256)

    def weights(p, left, right):
        for k, at in enumerate(spans):
            q, low = k * TILE // half, k * TILE % half
            value = dot_nn(left, right[:, at])
            for zz in range(4):
                for h in range(2):
                    for cc in range(NC):
                        base = zz * 64 + h * 32 + cc * 8
                        both = jnp.concatenate([value[base : base + 8], value[base + 16 : base + 24]], axis=0)
                        part[cc, p * 4 + zz, h, q, :, low : low + TILE] = both.astype(BF16)

    hidden_grad_wide = jnp.zeros((rows, 256), F32)
    for k, at in enumerate(spans):
        low = dot_nt(grad_out, wo[at, :]).astype(BF16)
        gc[:, at] = low
        gate = low.astype(F32) * x[:, at].astype(F32)
        bias[k * TILE // half, :, k * TILE % half : k * TILE % half + TILE] = jnp.sum(gate, axis=0, keepdims=True)
        gate_low = gate.astype(BF16)
        ggl[:, at] = gate_low
        hidden_grad_wide = hidden_grad_wide + dot_nt(gate_low, wu[:, at])
    hidden_grad = hidden_grad_wide.astype(BF16)
    bias_pair = remote(bias.at[1 - c], b_pair, bp_s, bp_r, partner)
    bias_pair.start()
    weights(2, grad_out.astype(F32).T.astype(BF16), cr)
    weights(1, hidden_t, ggl)
    weights(0, hidden_grad.astype(F32).T.astype(BF16), x)

    def chunk(offset, direction):
        return (z + direction * offset + NZ) % NZ

    pieces = []
    for k, offset in enumerate(NEED):
        pieces.append(
            remote(part.at[1 - c, chunk(offset, -sign)], pair.at[k], p_s.at[k], p_r.at[k], partner)
        )
        pieces[-1].start()

    bias_z = []
    bias_pair.wait_recv()
    b_z[z] = bias[c] + b_pair[...]
    for j in range(1, NZ):
        copy = remote(b_z.at[z], b_z.at[z], bz_s.at[j], bz_r.at[j], shard_at((z + j) % NZ, yl, c))
        copy.start()
        bias_z.append(copy)

    for k, at in enumerate(spans):
        value = gc[:, at].astype(F32) * fac[:, at] + dot_nt(hidden_grad, wd[at, :])
        low = value.astype(BF16)
        for a in range(TOWERS):
            for j in range(TILE // EMB):
                gi[a, k * (TILE // EMB) + j] = low[a * 32 : (a + 1) * 32, j * EMB : (j + 1) * EMB]
    second = []
    for i in order:
        dest = tower_at(i)
        second.append(remote(gi.at[dest], out_f.at[t], a2_s.at[i], a2_r.at[i], {"tower": dest}))
        second[-1].start()
    keep = pltpu.make_async_copy(gi.at[t], out_f.at[t], in_sem.at[6])
    keep.start()

    ahead = shard_at((z + sign + NZ) % NZ, yl, c)
    behind = shard_at((z - sign + NZ) % NZ, yl, c)

    def local_sum(k, h, q):
        return part[c, chunk(NEED[k], sign), h, q].astype(F32) + pair[k, h, q].astype(F32)

    arms = {
        "long": (long_s, long_r, l_s, l_r, ahead, LONG),
        "short": (short_s, short_r, s_s, s_r, behind, SHORT),
    }
    sent = {}
    bias_y = []
    for step in range(LONG):
        for name in ("long", "short"):
            if step < arms[name][5]:
                pieces[NEED.index(LONG - step if name == "long" else step - SHORT)].wait_recv()
        for h, q in SUBS:
            for name, (send_ref, recv_ref, send_sem, recv_sem, device, hops) in arms.items():
                if step >= hops:
                    continue
                value = local_sum(NEED.index(hops - step if name == "long" else step - hops), h, q)
                if step > 0:
                    sent[name, step - 1, h, q].wait_recv()
                    value = value + recv_ref[step - 1, h, q].astype(F32)
                send_ref[step, h, q] = value.astype(BF16)
                copy = remote(
                    send_ref.at[step, h, q], recv_ref.at[step, h, q],
                    send_sem.at[step, h * 2 + q], recv_sem.at[step, h * 2 + q], device,
                )
                copy.start()
                sent[name, step, h, q] = copy
        if step == 3:
            for copy in bias_z:
                copy.wait_recv()
            column = b_z[0]
            for k in range(1, NZ):
                column = column + b_z[k]
            b_y[yl] = column
            for j in range(1, NYL):
                copy = remote(b_y.at[yl], b_y.at[yl], by_s.at[j], by_r.at[j], shard_at(z, (yl + j) % NYL, c))
                copy.start()
                bias_y.append(copy)

    pieces[len(NEED) - 1].wait_recv()
    for h in range(2):
        halves = []
        for q in range(2):
            value = local_sum(len(NEED) - 1, h, q)
            sent["short", SHORT - 1, h, q].wait_recv()
            value = value + short_r[SHORT - 1, h, q].astype(F32)
            sent["long", LONG - 1, h, q].wait_recv()
            halves.append(value + long_r[LONG - 1, h, q].astype(F32))
        for yy in range(2):
            eight = [value[yy * 8 : (yy + 1) * 8] for value in halves]
            for q in range(2):
                mine[h * 2 + yy, :, q * half : (q + 1) * half] = eight[q]
            y_s[h * 2 + yy] = jnp.concatenate(eight, axis=0).astype(BF16)
    last = []
    for j in range(1, NYL):
        to = (yl + j) % NYL
        copy = remote(y_s.at[to], y_r.at[j - 1], ys_s.at[j], ys_r.at[j], shard_at(z, to, c))
        copy.start()
        last.append(copy)

    for copy in bias_y:
        copy.wait_recv()
    total = (b_y[0] + b_y[1]) + (b_y[2] + b_y[3])
    b_half[...] = total
    bias_final = remote(b_half, b_other, bf_s, bf_r, partner)
    bias_final.start()
    out_b[:, pl.ds(pl.multiple_of(c * half, half), half)] = total

    value = mine[yl]
    for copy in last:
        copy.wait_recv()
    for j in range(NYL - 1):
        got = y_r[j].astype(F32)
        value = value + jnp.concatenate([got[:8], got[8:]], axis=1)
    out_w[...] = value * scale

    bias_final.wait_recv()
    out_b[:, pl.ds(pl.multiple_of((1 - c) * half, half), half)] = b_other[...]

    keep.wait()
    for copy in second:
        copy.wait_recv()
    for copy in first + second + pieces + list(sent.values()) + bias_y + bias_z + last + [bias_pair, bias_final]:
        copy.wait_send()


def place_kernel(assign_ref, f_ref, w_ref, b_ref, out_f, out_w, out_b):
    for k in range(f_ref.shape[0]):
        out_f[:, pl.ds(pl.multiple_of(assign_ref[k] * EMB, EMB), EMB)] = f_ref[k]
    out_w[...] = w_ref[...]
    out_b[...] = b_ref[...]


def body(out_grad, pooled, down_proj, up_proj, cross_bias, out_proj, assign):
    rows, width = pooled.shape[1:]
    any_space = pl.BlockSpec(memory_space=pl.ANY)
    vmem = pl.BlockSpec(memory_space=pltpu.VMEM)
    scale = 1.0 / math.sqrt(rows * lax.axis_size("shard"))
    dma = pltpu.SemaphoreType.DMA
    half = width // 2
    moved, weights, bias = pl.pallas_call(
        functools.partial(main_kernel, scale),
        out_shape=(
            jax.ShapeDtypeStruct((TOWERS, width // EMB, 32, EMB), BF16),
            jax.ShapeDtypeStruct((8, width), F32),
            jax.ShapeDtypeStruct((1, width), F32),
        ),
        in_specs=[any_space] * 6,
        out_specs=(any_space, vmem, vmem),
        scratch_shapes=[
            pltpu.VMEM((rows, width), BF16),
            pltpu.VMEM((width, 256), BF16),
            pltpu.VMEM((256, width), BF16),
            pltpu.VMEM((width, 256), BF16),
            pltpu.VMEM((1, width), F32),
            pltpu.VMEM((TOWERS, 32, 256), BF16),
            pltpu.VMEM((rows, width), F32),
            pltpu.VMEM((rows, width), BF16),
            pltpu.VMEM((rows, width), BF16),
            pltpu.VMEM((rows, width), BF16),
            pltpu.VMEM((TOWERS, width // EMB, 32, EMB), BF16),
            pltpu.VMEM((NC, NZ, 2, 2, 16, half), BF16),
            pltpu.VMEM((NZ, 2, 2, 16, half), BF16),
            pltpu.VMEM((LONG, 2, 2, 16, half), BF16),
            pltpu.VMEM((LONG, 2, 2, 16, half), BF16),
            pltpu.VMEM((SHORT, 2, 2, 16, half), BF16),
            pltpu.VMEM((SHORT, 2, 2, 16, half), BF16),
            pltpu.VMEM((TOWERS, 32, 256), BF16),
            pltpu.VMEM((NYL, 8, width), F32),
            pltpu.VMEM((NYL, 16, half), BF16),
            pltpu.VMEM((NYL - 1, 16, half), BF16),
            pltpu.VMEM((2, 1, half), F32),
            pltpu.VMEM((1, half), F32),
            pltpu.VMEM((NYL, 1, half), F32),
            pltpu.VMEM((NZ, 1, half), F32),
            pltpu.VMEM((1, half), F32),
            pltpu.VMEM((1, half), F32),
            dma((7,)),
            dma((TOWERS,)),
            dma((TOWERS,)), dma((TOWERS,)), dma((TOWERS,)), dma((TOWERS,)),
            dma((NZ,)), dma((NZ,)),
            dma((LONG, 4)), dma((LONG, 4)), dma((SHORT, 4)), dma((SHORT, 4)),
            dma((NYL,)), dma((NYL,)),
            dma, dma, dma((NYL,)), dma((NYL,)), dma((NZ,)), dma((NZ,)), dma, dma,
        ],
        compiler_params=pltpu.CompilerParams(
            collective_id=0, has_side_effects=True, vmem_limit_bytes=65000 * 1024
        ),
        name="tower_backward",
    )(out_grad, pooled[0], down_proj[0], up_proj[0], out_proj[0], cross_bias)
    feature_grad, weight_grad, bias_grad = pl.pallas_call(
        place_kernel,
        out_shape=(
            jax.ShapeDtypeStruct((32, TOWERS * width), BF16),
            jax.ShapeDtypeStruct((8, width), F32),
            jax.ShapeDtypeStruct((1, width), F32),
        ),
        in_specs=[pl.BlockSpec(memory_space=pltpu.SMEM), vmem, vmem, vmem],
        out_specs=(vmem, vmem, vmem),
        name="place_columns",
    )(assign, moved.reshape(TOWERS * (width // EMB), 32, EMB), weights, bias)
    return (feature_grad, weight_grad[None], bias_grad)


def solution(mesh):
    placed = (
        P(("tower", "shard"), None),
        P("tower", "shard", None),
        P("tower", None, None),
        P("tower", None, None),
        P("tower", None),
        P("tower", None, None),
        P(),
    )
    return jax.shard_map(
        body,
        mesh=mesh,
        in_specs=placed,
        out_specs=(P(("tower", "shard"), None), P("tower", "shard", None), P("tower", None)),
        check_vma=False,
    )
```

```python
import functools
import math

import jax
import jax.numpy as jnp
from jax import lax
from jax.experimental import pallas as pl
from jax.experimental.pallas import tpu as pltpu
from jax.sharding import PartitionSpec as P

MESH = pl.DeviceIdType.MESH
F32 = jnp.float32
BF16 = jnp.bfloat16
NX, NYH, NZ, NYL, NC = 4, 2, 12, 4, 2
TOWERS = NX * NYH
EMB = 128
TILE = 512
LONG, SHORT = 6, 5
SUBS = ((0, 0), (0, 1), (1, 0), (1, 1))
NEED = (6, -5, 5, -4, 4, -3, 3, -2, 2, -1, 1, 0)


def dot_nn(a, b):
    return jnp.dot(a, b, preferred_element_type=F32)


def dot_nt(a, b):
    return lax.dot_general(a, b, (((1,), (1,)), ((), ())), preferred_element_type=F32)


def remote(src, dst, send, recv, device):
    return pltpu.make_async_remote_copy(
        src_ref=src, dst_ref=dst, send_sem=send, recv_sem=recv, device_id=device, device_id_type=MESH
    )


def main_kernel(
    scale,
    og_h, x_h, wd_h, wu_h, wo_h, cb_h,
    out_f, out_w, out_b,
    x, wd, wu, wo, cb, go, fac, cr, gc, ggl, gi, part, pair, long_s, long_r, short_s, short_r,
    og, mine, y_s, y_r, bias, b_pair, b_y, b_z, b_half, b_other,
    in_sem, og_sem, a1_s, a1_r, a2_s, a2_r, p_s, p_r, l_s, l_r, s_s, s_r, ys_s, ys_r,
    bp_s, bp_r, by_s, by_r, bz_s, bz_r, bf_s, bf_r,
):
    t = lax.axis_index("tower")
    s = lax.axis_index("shard")
    yh, xx = t // NX, t % NX
    z, yl, c = s // (NYL * NC), (s // NC) % NYL, s % NC
    sign = 1 - 2 * c
    rows, width = x.shape
    tiles = width // TILE
    half = width // 2

    def tower_at(i):
        return ((yh + i // NX) % NYH) * NX + (xx + i % NX) % NX

    def shard_at(zz, yy, cc):
        return {"shard": (zz * NYL + yy) * NC + cc}

    order = (6, 5, 7, 4, 2, 1, 3)
    partner = shard_at(z, yl, 1 - c)
    peers = [{"tower": tower_at(i)} for i in order]
    peers.append(partner)
    peers += [shard_at(z, (yl + j) % NYL, c) for j in range(1, NYL)]
    peers += [shard_at((z + j) % NZ, yl, c) for j in range(1, NZ)]

    barrier = pltpu.get_barrier_semaphore()
    for peer in peers:
        pl.semaphore_signal(barrier, inc=1, device_id=peer, device_id_type=MESH)

    loads = [
        pltpu.make_async_copy(src, dst, in_sem.at[k])
        for k, (src, dst) in enumerate(((x_h, x), (wd_h, wd), (wu_h, wu), (cb_h, cb), (wo_h, wo)))
    ]
    own = pltpu.make_async_copy(
        og_h.at[:, pl.ds(pl.multiple_of(t * 256, 256), 256)], go.at[t], in_sem.at[5]
    )
    stage = []
    for i in order:
        dest = tower_at(i)
        stage.append(
            pltpu.make_async_copy(og_h.at[:, pl.ds(pl.multiple_of(dest * 256, 256), 256)], og.at[dest], og_sem.at[i])
        )
        stage[-1].start()
    own.start()
    for load in loads:
        load.start()
    for copy in stage:
        copy.wait()
    pl.semaphore_wait(barrier, len(peers))

    first = []
    for i in order:
        dest = tower_at(i)
        first.append(remote(og.at[dest], go.at[t], a1_s.at[i], a1_r.at[i], {"tower": dest}))
        first[-1].start()

    loads[0].wait()
    loads[1].wait()
    hidden_wide = dot_nn(x[...], wd[...]).astype(BF16)
    hidden_t = hidden_wide.astype(F32).T.astype(BF16)
    loads[2].wait()
    loads[3].wait()

    spans = [pl.ds(k * TILE, TILE) for k in range(tiles)]
    for at in spans:
        factor = dot_nn(hidden_wide, wu[:, at]) + cb[:, at] + 1.0
        fac[:, at] = factor
        cr[:, at] = (x[:, at].astype(F32) * factor).astype(BF16)
    loads[4].wait()
    own.wait()
    for copy in first:
        copy.wait_recv()
    grad_out = go[...].reshape(rows, 256)

    def weights(p, left, right):
        for k, at in enumerate(spans):
            q, low = k * TILE // half, k * TILE % half
            value = dot_nn(left, right[:, at])
            for zz in range(4):
                for h in range(2):
                    for cc in range(NC):
                        base = zz * 64 + h * 32 + cc * 8
                        both = jnp.concatenate([value[base : base + 8], value[base + 16 : base + 24]], axis=0)
                        part[cc, p * 4 + zz, h, q, :, low : low + TILE] = both.astype(BF16)

    hidden_grad_wide = jnp.zeros((rows, 256), F32)
    for k, at in enumerate(spans):
        low = dot_nt(grad_out, wo[at, :]).astype(BF16)
        gc[:, at] = low
        gate = low.astype(F32) * x[:, at].astype(F32)
        bias[k * TILE // half, :, k * TILE % half : k * TILE % half + TILE] = jnp.sum(gate, axis=0, keepdims=True)
        gate_low = gate.astype(BF16)
        ggl[:, at] = gate_low
        hidden_grad_wide = hidden_grad_wide + dot_nt(gate_low, wu[:, at])
    hidden_grad = hidden_grad_wide.astype(BF16)
    bias_pair = remote(bias.at[1 - c], b_pair, bp_s, bp_r, partner)
    bias_pair.start()
    weights(2, grad_out.astype(F32).T.astype(BF16), cr)
    weights(1, hidden_t, ggl)
    weights(0, hidden_grad.astype(F32).T.astype(BF16), x)

    def chunk(offset, direction):
        return (z + direction * offset + NZ) % NZ

    pieces = []
    for k, offset in enumerate(NEED):
        pieces.append(
            remote(part.at[1 - c, chunk(offset, -sign)], pair.at[k], p_s.at[k], p_r.at[k], partner)
        )
        pieces[-1].start()

    bias_y = []
    bias_pair.wait_recv()
    b_y[yl] = bias[c] + b_pair[...]
    for j in range(1, NYL):
        copy = remote(b_y.at[yl], b_y.at[yl], by_s.at[j], by_r.at[j], shard_at(z, (yl + j) % NYL, c))
        copy.start()
        bias_y.append(copy)

    for k, at in enumerate(spans):
        value = gc[:, at].astype(F32) * fac[:, at] + dot_nt(hidden_grad, wd[at, :])
        low = value.astype(BF16)
        for a in range(TOWERS):
            for j in range(TILE // EMB):
                gi[a, k * (TILE // EMB) + j] = low[a * 32 : (a + 1) * 32, j * EMB : (j + 1) * EMB]
    second = []
    for i in order:
        dest = tower_at(i)
        second.append(remote(gi.at[dest], out_f.at[t], a2_s.at[i], a2_r.at[i], {"tower": dest}))
        second[-1].start()
    keep = pltpu.make_async_copy(gi.at[t], out_f.at[t], in_sem.at[6])
    keep.start()

    ahead = shard_at((z + sign + NZ) % NZ, yl, c)
    behind = shard_at((z - sign + NZ) % NZ, yl, c)

    def local_sum(k, h, q):
        return part[c, chunk(NEED[k], sign), h, q].astype(F32) + pair[k, h, q].astype(F32)

    arms = {
        "long": (long_s, long_r, l_s, l_r, ahead, LONG),
        "short": (short_s, short_r, s_s, s_r, behind, SHORT),
    }
    sent = {}
    bias_z = []
    for step in range(LONG):
        for name in ("long", "short"):
            if step < arms[name][5]:
                pieces[NEED.index(LONG - step if name == "long" else step - SHORT)].wait_recv()
        for h, q in SUBS:
            for name, (send_ref, recv_ref, send_sem, recv_sem, device, hops) in arms.items():
                if step >= hops:
                    continue
                value = local_sum(NEED.index(hops - step if name == "long" else step - hops), h, q)
                if step > 0:
                    sent[name, step - 1, h, q].wait_recv()
                    value = value + recv_ref[step - 1, h, q].astype(F32)
                send_ref[step, h, q] = value.astype(BF16)
                copy = remote(
                    send_ref.at[step, h, q], recv_ref.at[step, h, q],
                    send_sem.at[step, h * 2 + q], recv_sem.at[step, h * 2 + q], device,
                )
                copy.start()
                sent[name, step, h, q] = copy
        if step == 3:
            for copy in bias_y:
                copy.wait_recv()
            b_z[z] = (b_y[0] + b_y[1]) + (b_y[2] + b_y[3])

    for j in range(1, NZ):
        copy = remote(b_z.at[z], b_z.at[z], bz_s.at[j], bz_r.at[j], shard_at((z + j) % NZ, yl, c))
        copy.start()
        bias_z.append(copy)
    pieces[len(NEED) - 1].wait_recv()
    for h in range(2):
        halves = []
        for q in range(2):
            value = local_sum(len(NEED) - 1, h, q)
            sent["short", SHORT - 1, h, q].wait_recv()
            value = value + short_r[SHORT - 1, h, q].astype(F32)
            sent["long", LONG - 1, h, q].wait_recv()
            halves.append(value + long_r[LONG - 1, h, q].astype(F32))
        for yy in range(2):
            eight = [value[yy * 8 : (yy + 1) * 8] for value in halves]
            for q in range(2):
                mine[h * 2 + yy, :, q * half : (q + 1) * half] = eight[q]
            y_s[h * 2 + yy] = jnp.concatenate(eight, axis=0).astype(BF16)
    last = []
    for j in range(1, NYL):
        to = (yl + j) % NYL
        copy = remote(y_s.at[to], y_r.at[j - 1], ys_s.at[j], ys_r.at[j], shard_at(z, to, c))
        copy.start()
        last.append(copy)

    for copy in bias_z:
        copy.wait_recv()
    total = b_z[0]
    for k in range(1, NZ):
        total = total + b_z[k]
    b_half[...] = total
    bias_final = remote(b_half, b_other, bf_s, bf_r, partner)
    bias_final.start()
    out_b[:, pl.ds(pl.multiple_of(c * half, half), half)] = total

    value = mine[yl]
    for copy in last:
        copy.wait_recv()
    for j in range(NYL - 1):
        got = y_r[j].astype(F32)
        value = value + jnp.concatenate([got[:8], got[8:]], axis=1)
    out_w[...] = value * scale

    bias_final.wait_recv()
    out_b[:, pl.ds(pl.multiple_of((1 - c) * half, half), half)] = b_other[...]

    keep.wait()
    for copy in second:
        copy.wait_recv()
    for copy in first + second + pieces + list(sent.values()) + bias_y + bias_z + last + [bias_pair, bias_final]:
        copy.wait_send()


def place_kernel(assign_ref, f_ref, w_ref, b_ref, out_f, out_w, out_b):
    for k in range(f_ref.shape[0]):
        out_f[:, pl.ds(pl.multiple_of(assign_ref[k] * EMB, EMB), EMB)] = f_ref[k]
    out_w[...] = w_ref[...]
    out_b[...] = b_ref[...]


def body(out_grad, pooled, down_proj, up_proj, cross_bias, out_proj, assign):
    rows, width = pooled.shape[1:]
    any_space = pl.BlockSpec(memory_space=pl.ANY)
    vmem = pl.BlockSpec(memory_space=pltpu.VMEM)
    scale = 1.0 / math.sqrt(rows * lax.axis_size("shard"))
    dma = pltpu.SemaphoreType.DMA
    half = width // 2
    moved, weights, bias = pl.pallas_call(
        functools.partial(main_kernel, scale),
        out_shape=(
            jax.ShapeDtypeStruct((TOWERS, width // EMB, 32, EMB), BF16),
            jax.ShapeDtypeStruct((8, width), F32),
            jax.ShapeDtypeStruct((1, width), F32),
        ),
        in_specs=[any_space] * 6,
        out_specs=(any_space, vmem, vmem),
        scratch_shapes=[
            pltpu.VMEM((rows, width), BF16),
            pltpu.VMEM((width, 256), BF16),
            pltpu.VMEM((256, width), BF16),
            pltpu.VMEM((width, 256), BF16),
            pltpu.VMEM((1, width), F32),
            pltpu.VMEM((TOWERS, 32, 256), BF16),
            pltpu.VMEM((rows, width), F32),
            pltpu.VMEM((rows, width), BF16),
            pltpu.VMEM((rows, width), BF16),
            pltpu.VMEM((rows, width), BF16),
            pltpu.VMEM((TOWERS, width // EMB, 32, EMB), BF16),
            pltpu.VMEM((NC, NZ, 2, 2, 16, half), BF16),
            pltpu.VMEM((NZ, 2, 2, 16, half), BF16),
            pltpu.VMEM((LONG, 2, 2, 16, half), BF16),
            pltpu.VMEM((LONG, 2, 2, 16, half), BF16),
            pltpu.VMEM((SHORT, 2, 2, 16, half), BF16),
            pltpu.VMEM((SHORT, 2, 2, 16, half), BF16),
            pltpu.VMEM((TOWERS, 32, 256), BF16),
            pltpu.VMEM((NYL, 8, width), F32),
            pltpu.VMEM((NYL, 16, half), BF16),
            pltpu.VMEM((NYL - 1, 16, half), BF16),
            pltpu.VMEM((2, 1, half), F32),
            pltpu.VMEM((1, half), F32),
            pltpu.VMEM((NYL, 1, half), F32),
            pltpu.VMEM((NZ, 1, half), F32),
            pltpu.VMEM((1, half), F32),
            pltpu.VMEM((1, half), F32),
            dma((7,)),
            dma((TOWERS,)),
            dma((TOWERS,)), dma((TOWERS,)), dma((TOWERS,)), dma((TOWERS,)),
            dma((NZ,)), dma((NZ,)),
            dma((LONG, 4)), dma((LONG, 4)), dma((SHORT, 4)), dma((SHORT, 4)),
            dma((NYL,)), dma((NYL,)),
            dma, dma, dma((NYL,)), dma((NYL,)), dma((NZ,)), dma((NZ,)), dma, dma,
        ],
        compiler_params=pltpu.CompilerParams(
            collective_id=0, has_side_effects=True, vmem_limit_bytes=65000 * 1024
        ),
        name="tower_backward",
    )(out_grad, pooled[0], down_proj[0], up_proj[0], out_proj[0], cross_bias)
    feature_grad, weight_grad, bias_grad = pl.pallas_call(
        place_kernel,
        out_shape=(
            jax.ShapeDtypeStruct((32, TOWERS * width), BF16),
            jax.ShapeDtypeStruct((8, width), F32),
            jax.ShapeDtypeStruct((1, width), F32),
        ),
        in_specs=[pl.BlockSpec(memory_space=pltpu.SMEM), vmem, vmem, vmem],
        out_specs=(vmem, vmem, vmem),
        name="place_columns",
    )(assign, moved.reshape(TOWERS * (width // EMB), 32, EMB), weights, bias)
    return (feature_grad, weight_grad[None], bias_grad)


def solution(mesh):
    placed = (
        P(("tower", "shard"), None),
        P("tower", "shard", None),
        P("tower", None, None),
        P("tower", None, None),
        P("tower", None),
        P("tower", None, None),
        P(),
    )
    return jax.shard_map(
        body,
        mesh=mesh,
        in_specs=placed,
        out_specs=(P(("tower", "shard"), None), P("tower", "shard", None), P("tower", None)),
        check_vma=False,
    )
```
